32 devices in a mesh: wide: 16 (over z, y, core), narrow: 2 (over x).
Axes of the slice: x: 2, y: 2, z: 4, core: 2. Of those that a mesh axis runs over, the one named last changes fastest.
Arguments:
- left: bfloat16 [64, 1024, 256], P(None, 'wide', 'narrow'), may hold values from -6 to 6
- right: bfloat16 [64, 1024, 256], P(None, 'wide', 'narrow'), may hold values from -6 to 6
- bond_signs: int32 [4, 8, 1024, 256], P(None, None, 'wide', 'narrow'), may hold values from 0 to 1
- hop: float32 [4, 4], replicated, may hold values from 0.2 to 1
Outputs:
- moments: float32 [16, 64, 64], P(None, 'wide', 'narrow')
The draws below stay inside these ranges and needn't reach their ends.
All inputs are finite; a program needn't handle non-finite values.
Results may differ from the reference program's by a relative error of at most 0.004.
Values may be sent and summed in bfloat16 or wider, within the bound.
No kernel may reach another device: no remote copies, remote signals or barrier semaphores. Data moves between devices by JAX's collectives and lax.ppermute only.
A program may use at most 64 MiB of HBM per device.

```python
import math
import jax
import jax.numpy as jnp
from jax import lax

NL = 64
NR = 64
OPS = 4
RANGE = 4
NX = 1024
NY = 256


def touch_ends(drawn, rng, least, high):
    spot = [jax.random.randint(jax.random.fold_in(rng, axis), (), 0, length) for axis, length in enumerate(drawn.shape)]
    main_axis = drawn.shape.index(max(drawn.shape))
    beside = spot[:main_axis] + [(spot[main_axis] + 1) % drawn.shape[main_axis]] + spot[main_axis + 1:]
    return drawn.at[tuple(spot)].set(least).at[tuple(beside)].set(high)


def block_levels(rng, shape, pieces, low, high):
    level, own = 1.0, jax.random.fold_in(rng, 6)
    for position, parts in pieces:
        heights = jnp.exp(jax.random.uniform(jax.random.fold_in(own, position), (parts,), jnp.float32, low / len(pieces), high / len(pieces)))
        level = level * jnp.repeat(heights, shape[position] // parts).reshape([-1 if axis == position else 1 for axis in range(len(shape))])
    return level


def gaussian(key, extent, deviation, limit, split=(), kind=jnp.bfloat16):
    loudness = block_levels(key, extent, split, -0.22, 0.18) if split else 1.0
    drawn = jax.random.normal(key, extent, jnp.float32) * deviation * loudness
    return jnp.minimum(jnp.maximum(drawn, -limit), limit).astype(kind)


def setup_inputs(seed: int = 0) -> dict:
    seeds = jax.random.split(jax.random.key(seed), 5)
    left = gaussian(seeds[0], (NL, NX, NY), 1.0, 6.0, ((1, 16), (2, 2)))
    right = gaussian(seeds[1], (NR, NX, NY), 1.0, 6.0, ((1, 16), (2, 2)))
    bond_signs = touch_ends(jax.random.randint(seeds[2], (OPS, 2 * RANGE, NX, NY), 0, 2), jax.random.fold_in(seeds[2], 1), 0, 1).astype(jnp.int32)
    hop = jnp.clip(jnp.exp(jax.random.uniform(seeds[3], (OPS, RANGE), jnp.float32, math.log(0.2), math.log(1.0))), 0.2, 1.0)
    return dict(left=left, right=right, bond_signs=bond_signs, hop=hop)


def current_full(vectors, sign_bits, coefficient, direction):
    signs_float = (2 * sign_bits - 1).astype(jnp.float32)
    summed = jnp.zeros(vectors.shape, jnp.float32)
    for index in range(RANGE):
        offset = index + 1
        ahead = jnp.roll(vectors, -offset, axis=direction).astype(jnp.float32)
        behind = jnp.roll(vectors, offset, axis=direction).astype(jnp.float32)
        summed = summed + coefficient[index] * (signs_float[index] * ahead - signs_float[RANGE + index] * behind)
    return summed

def adjoint_full(vectors, sign_bits, coefficient, direction):
    signs_float = (2 * sign_bits - 1).astype(jnp.float32)
    values = vectors.astype(jnp.float32)
    summed = jnp.zeros(vectors.shape, jnp.float32)
    for index in range(RANGE):
        offset = index + 1
        forward = jnp.roll(signs_float[index] * values, offset, axis=direction)
        backward = jnp.roll(signs_float[RANGE + index] * values, -offset, axis=direction)
        summed = summed + coefficient[index] * (forward - backward)
    return summed

def reference(left, right, bond_signs, hop):
    left_blocks = left.reshape(NL // 8, 8, NX, NY)
    right_blocks = right.reshape(NR // 8, 8, NX, NY)

    def right_block(block_right):
        first = jnp.stack([current_full(block_right, bond_signs[inner], hop[inner], 1 + inner % 2).astype(jnp.bfloat16) for inner in range(OPS)]).reshape(OPS * 8, NX * NY)

        def left_block(block_left):
            back = jnp.stack([adjoint_full(block_left, bond_signs[outer], hop[outer], 1 + outer % 2).astype(jnp.bfloat16) for outer in range(OPS)]).reshape(OPS * 8, NX * NY)
            return jnp.dot(back, first.T, preferred_element_type=jnp.float32)
        return lax.map(left_block, left_blocks)
    mapped = lax.map(right_block, right_blocks).reshape(NR // 8, NL // 8, OPS, 8, OPS, 8)
    moments = jnp.transpose(mapped, (2, 4, 1, 3, 0, 5)).reshape(OPS * OPS, NL, NR)
    return moments * jnp.float32(1.0 / math.sqrt(NX * NY))
```

```python
import math

import jax
import jax.numpy as jnp
from jax import lax
from jax.experimental import pallas as pl
from jax.experimental.pallas import tpu as pltpu
from jax.sharding import PartitionSpec as P

OPS = 4
RANGE = 4
TAPS = 2 * RANGE
EVEN = tuple(a for a in range(OPS) if a % 2 == 0)
ODD = tuple(a for a in range(OPS) if a % 2 == 1)
SUB = 8
LANES = 128
VMEM = pltpu.VMEM
F32 = jnp.float32
BF16 = jnp.bfloat16


def lane_index(shape):
    return lax.broadcasted_iota(jnp.int32, shape, len(shape) - 1)


def pack_kernel(parity, right, left, bonds, near, far, side, head, tail):
    count, rows, cols = right.shape
    even = parity[0] == 0
    group = LANES // TAPS

    def sign_of(a, index):
        return (2 * bonds[a, index] - 1).astype(F32)

    fields = [(right, count), (left, count)]
    slot = 0
    for ref, n in fields:
        @pl.loop(0, n)
        def _(v, ref=ref, slot=slot):
            at = pl.multiple_of((v + slot) * SUB, SUB)
            head[pl.ds(at, SUB), :] = ref[v, : 2 * SUB, :].astype(F32)[:SUB]
            tail[pl.ds(at, SUB), :] = ref[v, rows - 2 * SUB :, :].astype(F32)[SUB:]

        slot += n
    for a in EVEN:
        for index in range(TAPS):
            head[slot * SUB : slot * SUB + SUB, :] = (2 * bonds[a, index, :SUB, :] - 1).astype(F32)
            tail[slot * SUB : slot * SUB + SUB, :] = (2 * bonds[a, index, rows - SUB :, :] - 1).astype(F32)
            slot += 1
    for base in range(0, slot, 2 * SUB):
        for row in range(RANGE):
            def strip(ref, offset):
                parts = [ref[pl.ds((base + half * SUB) * SUB + offset, SUB, stride=SUB), :] for half in range(2)]
                return jnp.concatenate(parts, axis=0)

            low = strip(head, row)
            high = strip(tail, SUB - RANGE + row)
            near[row, base : base + 2 * SUB, :] = jnp.where(even, high, low).astype(BF16)
            far[row, base : base + 2 * SUB, :] = jnp.where(even, low, high).astype(BF16)

    lane = lane_index((rows, cols))
    for which, ref in enumerate((right, left)):
        for block in range(count // group):
            total = jnp.zeros((rows, cols), F32)
            for t in range(group):
                moved = pltpu.roll(ref[block * group + t].astype(F32), RANGE + TAPS * t, 1)
                total = jnp.where(lane // TAPS == t, moved, total)
            side[which * (count // group) + block] = total.astype(BF16)
    total = jnp.zeros((rows, cols), F32)
    for t in range(len(ODD) * TAPS):
        moved = pltpu.roll(sign_of(ODD[t // TAPS], t % TAPS), RANGE + TAPS * t, 1)
        total = jnp.where(lane // TAPS == t, moved, total)
    side[2 * (count // group)] = total.astype(BF16)


def main_kernel(widths, parity, hop, right, left, bonds, near, far, side, out,
                value, edge, coef, turned, acc, back_a, first_a, back_b, first_b):
    count, rows, cols = right.shape
    even = parity[0] == 0
    group = LANES // TAPS
    stride = rows + 2 * SUB
    lane = lane_index((SUB, cols))
    lane_all = lane_index((rows, cols))

    def outer(slab, row):
        low = jnp.where(even, far[row, slab, :].astype(F32), near[row, slab, :].astype(F32))
        high = jnp.where(even, near[row, slab, :].astype(F32), far[row, slab, :].astype(F32))
        return low, high

    for which, ref in enumerate((right, left)):
        @pl.loop(0, count)
        def _(v, which=which, ref=ref):
            value[which, pl.ds(pl.multiple_of(v * stride + SUB, SUB), rows), :] = ref[v].astype(F32)

        for base in range(0, count, 2 * SUB):
            for row in range(RANGE):
                low, high = outer(slice(which * count + base, which * count + base + 2 * SUB), row)
                for half in range(2):
                    at = (base + half * SUB) * stride + row
                    part = slice(half * SUB, half * SUB + SUB)
                    value[which, pl.ds(at + SUB - RANGE, SUB, stride=stride), :] = low[part]
                    value[which, pl.ds(at + SUB + rows, SUB, stride=stride), :] = high[part]

        @pl.loop(0, count // group)
        def _(block, which=which):
            packed = side[which * (count // group) + block].astype(F32)
            for t in range(group):
                at = pl.multiple_of((block * group + t) * rows, SUB)
                edge[which, pl.ds(at, rows), :] = pltpu.roll(packed, (LANES - RANGE - TAPS * t) % LANES, 1)

    for a in range(OPS):
        for index in range(TAPS):
            scale = hop[a, index % RANGE] * (1.0 if index < RANGE else -1.0)
            coef[a * TAPS + index, SUB : SUB + rows, :] = (2 * bonds[a, index] - 1).astype(F32) * scale
    for row in range(RANGE):
        low, high = outer(slice(2 * count, 2 * count + 2 * SUB), row)
        for slot in range(len(EVEN) * TAPS):
            a, index = EVEN[slot // TAPS], slot % TAPS
            scale = hop[a, index % RANGE] * (1.0 if index < RANGE else -1.0)
            where = SUB - RANGE + row if index < RANGE else SUB + rows + row
            source = low if index < RANGE else high
            coef[a * TAPS + index, where : where + 1, :] = source[slot : slot + 1] * scale
    packed = side[2 * (count // group)].astype(F32)
    for slot in range(len(ODD) * TAPS):
        a, index = ODD[slot // TAPS], slot % TAPS
        step = index % RANGE + 1
        scale = hop[a, index % RANGE] * (1.0 if index < RANGE else -1.0)
        beyond = pltpu.roll(packed, (LANES - RANGE - TAPS * slot) % LANES, 1) * scale
        inside = coef[a * TAPS + index, SUB : SUB + rows, :]
        if index < RANGE:
            turned[slot] = pltpu.roll(jnp.where(lane_all >= cols - step, beyond, inside), step, 1)
        else:
            turned[slot] = pltpu.roll(jnp.where(lane_all < step, beyond, inside), cols - step, 1)

    acc[...] = jnp.zeros_like(acc)

    def stencil(row, part, back, first):
        for which, target in ((0, first), (1, back)):
            factors = {}
            for a in range(OPS):
                for index in range(TAPS):
                    step = index % RANGE + 1
                    if which == 0:
                        source, at = coef.at[a * TAPS + index], row + SUB
                    elif a % 2 == 0:
                        source, at = coef.at[a * TAPS + index], row + SUB + (-step if index < RANGE else step)
                    else:
                        source, at = turned.at[ODD.index(a) * TAPS + index], row
                    factors[a, index] = source[pl.ds(at, SUB, stride=0), :]
            ahead = 1 if which == 0 else -1
            for pair in range(count // (2 * SUB)):
                sums = {a: [] for a in range(OPS)}
                for half in range(2):
                    first_vec = (2 * pair + half) * SUB
                    here = first_vec * stride + row + SUB
                    total = {}
                    for index in range(TAPS):
                        step = (index % RANGE + 1) * (ahead if index < RANGE else -ahead)
                        moved = value[which, pl.ds(here + step, SUB, stride=stride), :]
                        for a in EVEN:
                            term = factors[a, index] * moved
                            total[a] = term if index == 0 else total[a] + term
                    middle = value[which, pl.ds(here, SUB, stride=stride), :]
                    beyond = edge[which, pl.ds(first_vec * rows + row, SUB, stride=rows), :]
                    for index in range(TAPS):
                        step = (index % RANGE + 1) * (ahead if index < RANGE else -ahead)
                        inner = (lane < step) if step > 0 else (lane >= cols + step)
                        moved = pltpu.roll(jnp.where(inner, beyond, middle), (cols - step) % cols, 1)
                        for a in ODD:
                            term = factors[a, index] * moved
                            total[a] = term if index == 0 else total[a] + term
                    for a in range(OPS):
                        sums[a].append(total[a])
                for a in range(OPS):
                    at = a * count + pair * 2 * SUB
                    target[at : at + 2 * SUB, part * cols : part * cols + cols] = jnp.concatenate(sums[a], axis=0).astype(BF16)

    def product(back, first):
        acc[...] += lax.dot_general(back[...], first[...], (((1,), (1,)), ((), ())), preferred_element_type=F32)

    back_b[...] = jnp.zeros_like(back_b)
    first_b[...] = jnp.zeros_like(first_b)

    @pl.loop(0, rows // 4)
    def _(step):
        product(back_b, first_b)
        for part in range(2):
            stencil(step * 4 + part, part, back_a, first_a)
        product(back_a, first_a)
        for part in range(2):
            stencil(step * 4 + 2 + part, part, back_b, first_b)

    product(back_b, first_b)

    parts_left, parts_right = widths
    per_left, per_right = count // parts_left, count // parts_right
    size = OPS * count

    def order(parts, per, dim):
        new = lax.broadcasted_iota(jnp.int32, (size, size), dim)
        old = lax.broadcasted_iota(jnp.int32, (size, size), 1 - dim)
        part, rest = new // (OPS * per), new % (OPS * per)
        return jnp.where(old == (rest // per) * count + part * per + rest % per, 1.0, 0.0).astype(BF16)

    moved = jnp.dot(order(parts_left, per_left, 0), acc[...].astype(BF16), preferred_element_type=F32).astype(BF16)
    moved = jnp.dot(moved, order(parts_right, per_right, 1), preferred_element_type=F32).astype(BF16)
    if out.ndim == 2:
        out[...] = moved
    else:
        width = OPS * per_right
        for d in range(parts_left * parts_right):
            w, r = divmod(d, parts_right)
            out[d] = moved[w * OPS * per_left : (w + 1) * OPS * per_left, r * width : (r + 1) * width]


def sum_kernel(factor, got, out):
    total = jnp.sum(got[...].astype(F32), axis=0) * factor
    per_left, per_right = out.shape[1], out.shape[2]
    for a in range(OPS):
        for b in range(OPS):
            out[a * OPS + b] = total[a * per_left : (a + 1) * per_left, b * per_right : (b + 1) * per_right]


def swap(array, axis, pairs):
    return lax.ppermute(array, axis, pairs)


def on_device(left, right, bond_signs, hop):
    count, rows, cols = right.shape
    wide, narrow = lax.axis_size("wide"), lax.axis_size("narrow")
    group = LANES // TAPS
    blocks = 2 * (count // group) + 1
    edge_rows = 2 * count + len(EVEN) * TAPS
    parity = (lax.axis_index("wide") % 2).astype(jnp.int32).reshape(1)
    smem = pl.BlockSpec(memory_space=pltpu.SMEM)
    vmem = pl.BlockSpec(memory_space=pltpu.VMEM)

    near, far, side = pl.pallas_call(
        pack_kernel,
        out_shape=(
            jax.ShapeDtypeStruct((RANGE, edge_rows, cols), BF16),
            jax.ShapeDtypeStruct((RANGE, edge_rows, cols), BF16),
            jax.ShapeDtypeStruct((blocks, rows, cols), BF16),
        ),
        in_specs=[smem, vmem, vmem, vmem],
        out_specs=(vmem, vmem, vmem),
        scratch_shapes=[VMEM((edge_rows * SUB, cols), F32), VMEM((edge_rows * SUB, cols), F32)],
        name="pack",
    )(parity, right, left, bond_signs)

    far = swap(far, "wide", [(i, (i + 1) % wide if i % 2 else (i - 1) % wide) for i in range(wide)])
    near = swap(near, "wide", [(i, i ^ 1) for i in range(wide)])
    if narrow == 2:
        side = swap(side, "narrow", [(0, 1), (1, 0)])
    else:
        before = swap(side, "narrow", [(i, (i + 1) % narrow) for i in range(narrow)])
        after = swap(side, "narrow", [((i + 1) % narrow, i) for i in range(narrow)])
        side = jnp.where(lane_index(side.shape) % TAPS < RANGE, before, after)

    per_left, per_right = count // wide, count // narrow
    size = OPS * count
    direct = (OPS * per_right) % LANES == 0 and (OPS * per_left) % 16 == 0
    blocked = (wide * narrow, OPS * per_left, OPS * per_right)
    partial = pl.pallas_call(
        lambda *refs: main_kernel((wide, narrow), *refs),
        out_shape=jax.ShapeDtypeStruct(blocked if direct else (size, size), BF16),
        in_specs=[smem, smem] + [vmem] * 6,
        out_specs=vmem,
        scratch_shapes=[
            VMEM((2, count * (rows + 2 * SUB), cols), F32),
            VMEM((2, count * rows, cols), F32),
            VMEM((OPS * TAPS, rows + 2 * SUB, cols), F32),
            VMEM((len(ODD) * TAPS, rows, cols), F32),
            VMEM((size, size), F32),
        ] + [VMEM((size, 2 * cols), BF16)] * 4,
        name="moments",
    )(parity, hop, right, left, bond_signs, near, far, side)
    if not direct:
        partial = partial.reshape(wide, OPS * per_left, narrow, OPS * per_right).transpose(0, 2, 1, 3).reshape(blocked)
    got = lax.all_to_all(partial, ("wide", "narrow"), 0, 0, tiled=True)
    factor = 1.0 / math.sqrt(rows * cols * wide * narrow)
    return pl.pallas_call(
        lambda *refs: sum_kernel(factor, *refs),
        out_shape=jax.ShapeDtypeStruct((OPS * OPS, per_left, per_right), F32),
        in_specs=[vmem],
        out_specs=vmem,
        name="total",
    )(got)


def solution(mesh):
    in_specs = (
        P(None, "wide", "narrow"),
        P(None, "wide", "narrow"),
        P(None, None, "wide", "narrow"),
        P(),
    )
    out_specs = P(None, "wide", "narrow")
    return jax.shard_map(
        on_device, mesh=mesh, in_specs=in_specs, out_specs=out_specs, check_vma=False
    )
```

```python
import math

import jax
import jax.numpy as jnp
from jax import lax
from jax.experimental import pallas as pl
from jax.experimental.pallas import tpu as pltpu
from jax.sharding import PartitionSpec as P

OPS = 4
RANGE = 4
TAPS = 2 * RANGE
EVEN = tuple(a for a in range(OPS) if a % 2 == 0)
ODD = tuple(a for a in range(OPS) if a % 2 == 1)
SUB = 8
LANES = 128
VMEM = pltpu.VMEM
F32 = jnp.float32
BF16 = jnp.bfloat16


def lane_index(shape):
    return lax.broadcasted_iota(jnp.int32, shape, len(shape) - 1)


def pack_kernel(parity, right, left, bonds, near, far, side, head, tail):
    count, rows, cols = right.shape
    even = parity[0] == 0
    group = LANES // TAPS

    def sign_of(a, index):
        return (2 * bonds[a, index] - 1).astype(F32)

    fields = [(right, count), (left, count)]
    slot = 0
    for ref, n in fields:
        @pl.loop(0, n)
        def _(v, ref=ref, slot=slot):
            at = pl.multiple_of((v + slot) * SUB, SUB)
            head[pl.ds(at, SUB), :] = ref[v, : 2 * SUB, :].astype(F32)[:SUB]
            tail[pl.ds(at, SUB), :] = ref[v, rows - 2 * SUB :, :].astype(F32)[SUB:]

        slot += n
    for a in EVEN:
        for index in range(TAPS):
            head[slot * SUB : slot * SUB + SUB, :] = (2 * bonds[a, index, :SUB, :] - 1).astype(F32)
            tail[slot * SUB : slot * SUB + SUB, :] = (2 * bonds[a, index, rows - SUB :, :] - 1).astype(F32)
            slot += 1
    for base in range(0, slot, 2 * SUB):
        for row in range(RANGE):
            def strip(ref, offset):
                parts = [ref[pl.ds((base + half * SUB) * SUB + offset, SUB, stride=SUB), :] for half in range(2)]
                return jnp.concatenate(parts, axis=0)

            low = strip(head, row)
            high = strip(tail, SUB - RANGE + row)
            near[row, base : base + 2 * SUB, :] = jnp.where(even, high, low).astype(BF16)
            far[row, base : base + 2 * SUB, :] = jnp.where(even, low, high).astype(BF16)

    lane = lane_index((rows, cols))
    for which, ref in enumerate((right, left)):
        for block in range(count // group):
            total = jnp.zeros((rows, cols), F32)
            for t in range(group):
                moved = pltpu.roll(ref[block * group + t].astype(F32), RANGE + TAPS * t, 1)
                total = jnp.where(lane // TAPS == t, moved, total)
            side[which * (count // group) + block] = total.astype(BF16)
    total = jnp.zeros((rows, cols), F32)
    for t in range(len(ODD) * TAPS):
        moved = pltpu.roll(sign_of(ODD[t // TAPS], t % TAPS), RANGE + TAPS * t, 1)
        total = jnp.where(lane // TAPS == t, moved, total)
    side[2 * (count // group)] = total.astype(BF16)


def main_kernel(widths, parity, hop, right, left, bonds, near, far, side, out,
                value, rim, coef, band, mats, acc, back_a, first_a, back_b, first_b):
    count, rows, cols = right.shape
    even = parity[0] == 0
    group = LANES // TAPS
    blocks = count // group
    stride = rows + 2 * SUB + 1
    period = 2 * TAPS
    lane_all = lane_index((rows, cols))

    def scale_of(a, index):
        return hop[a, index % RANGE] * (1.0 if index < RANGE else -1.0)

    def outer(slab, row):
        low = jnp.where(even, far[row, slab, :].astype(F32), near[row, slab, :].astype(F32))
        high = jnp.where(even, near[row, slab, :].astype(F32), far[row, slab, :].astype(F32))
        return low, high

    for a in range(OPS):
        for index in range(TAPS):
            coef[a * TAPS + index, SUB : SUB + rows, :] = (2 * bonds[a, index] - 1).astype(F32) * scale_of(a, index)
    for row in range(RANGE):
        low, high = outer(slice(2 * count, 2 * count + 2 * SUB), row)
        for slot in range(len(EVEN) * TAPS):
            a, index = EVEN[slot // TAPS], slot % TAPS
            where = SUB - RANGE + row if index < RANGE else SUB + rows + row
            source = low if index < RANGE else high
            coef[a * TAPS + index, where : where + 1, :] = source[slot : slot + 1] * scale_of(a, index)

    inner_lane = lane_all % TAPS
    last = inner_lane < RANGE
    signs = side[2 * blocks].astype(F32)
    weights = {}
    for which in range(2):
        for a in ODD:
            for k in range(1, RANGE + 1):
                if which == 0:
                    tops = pltpu.roll(coef[a * TAPS + k - 1, SUB : SUB + rows, :], RANGE, 1)
                    bottoms = pltpu.roll(coef[a * TAPS + RANGE + k - 1, SUB : SUB + rows, :], RANGE, 1)
                else:
                    slot = ODD.index(a) * TAPS + k - 1
                    bottoms = pltpu.roll(signs, (k - TAPS * slot) % LANES, 1) * scale_of(a, k - 1)
                    tops = pltpu.roll(signs, (-k - TAPS * (slot + RANGE)) % LANES, 1) * scale_of(a, RANGE + k - 1)
                one = jnp.where(lane_all < RANGE, tops, bottoms)
                valid = ((lane_all < RANGE) & (lane_all + k >= RANGE)) | ((lane_all >= RANGE) & (lane_all - k < RANGE) & (lane_all < TAPS))
                one = jnp.where(valid, one, 0.0)
                for shift in (TAPS, 2 * TAPS, 4 * TAPS, 8 * TAPS):
                    one = one + pltpu.roll(one, shift, 1)
                weights[which, a, k] = one
        for block in range(blocks):
            packed = side[which * blocks + block].astype(F32)
            total = {}
            for k in range(1, RANGE + 1):
                moved = jnp.where(last, pltpu.roll(packed, LANES - k, 1), pltpu.roll(packed, k, 1))
                for a in ODD:
                    term = weights[which, a, k] * moved
                    total[a] = term if k == 1 else total[a] + term
            for a in ODD:
                band[which * blocks + block, ODD.index(a)] = total[a]

        ref = (right, left)[which]

        @pl.loop(0, blocks)
        def _(block, which=which, ref=ref):
            for o in range(len(ODD)):
                packed = band[which * blocks + block, o]
                for t in range(group):
                    moved = pltpu.roll(packed, (LANES - RANGE - TAPS * t) % LANES, 1)
                    moved = jnp.where((lane_all < RANGE) | (lane_all >= cols - RANGE), moved, 0.0)
                    rim[which, o, pl.ds((block * group + t) * (rows + 1), rows), :] = moved
            for t in range(group):
                v = block * group + t
                value[which, pl.ds(v * stride + SUB, rows), :] = ref[v].astype(F32)

        for base in range(0, count, 2 * SUB):
            for row in range(RANGE):
                low, high = outer(slice(which * count + base, which * count + base + 2 * SUB), row)
                for half in range(2):
                    at = (base + half * SUB) * stride + row
                    part = slice(half * SUB, half * SUB + SUB)
                    value[which, pl.ds(at + SUB - RANGE, SUB, stride=stride), :] = low[part]
                    value[which, pl.ds(at + SUB + rows, SUB, stride=stride), :] = high[part]

    acc[...] = jnp.zeros_like(acc)

    tile = (period, cols)
    gap = (lane_index(tile) - lax.broadcasted_iota(jnp.int32, tile, 0)) % period
    near_diagonal = lane_index((cols, cols)) - lax.broadcasted_iota(jnp.int32, (cols, cols), 0)
    within = jnp.where((near_diagonal >= -TAPS) & (near_diagonal < TAPS), 1.0, 0.0).astype(BF16)

    def matrices(row, slot):
        for a in ODD:
            total = jnp.zeros(tile, F32)
            for k in range(1, RANGE + 1):
                total = jnp.where(gap == period - k, coef[a * TAPS + k - 1, pl.ds(row + SUB, period, stride=0), :], total)
                total = jnp.where(gap == k, coef[a * TAPS + RANGE + k - 1, pl.ds(row + SUB, period, stride=0), :], total)
            high = total.astype(BF16)
            low = (total - high.astype(F32)).astype(BF16)
            o = ODD.index(a)
            for part, piece in enumerate((high, low)):
                mats[slot, part * cols : (part + 1) * cols, o * cols : (o + 1) * cols] = (
                    jnp.concatenate([piece] * (cols // period), axis=0) * within
                )

    def stencil(row, part, slot, back, first):
        matrices(row, slot)
        here_lanes = slice(part * cols, (part + 1) * cols)
        for which, target in ((0, first), (1, back)):
            middle = jnp.concatenate(
                [value[which, pl.ds(g * SUB * stride + row + SUB, SUB, stride=stride), :] for g in range(count // SUB)], axis=0
            ).astype(BF16)
            for o, a in enumerate(ODD):
                mine = slice(o * cols, (o + 1) * cols)
                dims = (((1,), (which,)), ((), ()))
                total = lax.dot_general(middle, mats[slot, :cols, mine], dims, preferred_element_type=F32)
                total = total + lax.dot_general(middle, mats[slot, cols:, mine], dims, preferred_element_type=F32)
                beyond = jnp.concatenate(
                    [rim[which, o, pl.ds(g * SUB * (rows + 1) + row, SUB, stride=rows + 1), :] for g in range(count // SUB)], axis=0
                )
                target[a * count : (a + 1) * count, here_lanes] = (total + beyond).astype(BF16)
            factors = {}
            for a in EVEN:
                for index in range(TAPS):
                    step = index % RANGE + 1
                    at = row + SUB if which == 0 else row + SUB + (-step if index < RANGE else step)
                    factors[a, index] = coef[a * TAPS + index, pl.ds(at, SUB, stride=0), :]
            ahead = 1 if which == 0 else -1
            for pair in range(count // (2 * SUB)):
                sums = {a: [] for a in EVEN}
                for half in range(2):
                    here = (2 * pair + half) * SUB * stride + row + SUB
                    total = {}
                    for index in range(TAPS):
                        step = (index % RANGE + 1) * (ahead if index < RANGE else -ahead)
                        moved = value[which, pl.ds(here + step, SUB, stride=stride), :]
                        for a in EVEN:
                            term = factors[a, index] * moved
                            total[a] = term if index == 0 else total[a] + term
                    for a in EVEN:
                        sums[a].append(total[a])
                for a in EVEN:
                    at = a * count + pair * 2 * SUB
                    target[at : at + 2 * SUB, here_lanes] = jnp.concatenate(sums[a], axis=0).astype(BF16)

    def product(back, first):
        acc[...] += lax.dot_general(back[...], first[...], (((1,), (1,)), ((), ())), preferred_element_type=F32)

    back_b[...] = jnp.zeros_like(back_b)
    first_b[...] = jnp.zeros_like(first_b)

    @pl.loop(0, rows // 4)
    def _(step):
        product(back_b, first_b)
        for part in range(2):
            stencil(step * 4 + part, part, part, back_a, first_a)
        product(back_a, first_a)
        for part in range(2):
            stencil(step * 4 + 2 + part, part, 2 + part, back_b, first_b)

    product(back_b, first_b)

    parts_left, parts_right = widths
    per_left, per_right = count // parts_left, count // parts_right
    size = OPS * count

    def order(parts, per, dim):
        new = lax.broadcasted_iota(jnp.int32, (size, size), dim)
        old = lax.broadcasted_iota(jnp.int32, (size, size), 1 - dim)
        part, rest = new // (OPS * per), new % (OPS * per)
        return jnp.where(old == (rest // per) * count + part * per + rest % per, 1.0, 0.0).astype(BF16)

    moved = jnp.dot(order(parts_left, per_left, 0), acc[...].astype(BF16), preferred_element_type=F32).astype(BF16)
    moved = jnp.dot(moved, order(parts_right, per_right, 1), preferred_element_type=F32).astype(BF16)
    if out.ndim == 2:
        out[...] = moved
    else:
        width = OPS * per_right
        for d in range(parts_left * parts_right):
            w, r = divmod(d, parts_right)
            out[d] = moved[w * OPS * per_left : (w + 1) * OPS * per_left, r * width : (r + 1) * width]


def sum_kernel(factor, got, out):
    total = jnp.sum(got[...].astype(F32), axis=0) * factor
    per_left, per_right = out.shape[1], out.shape[2]
    for a in range(OPS):
        for b in range(OPS):
            out[a * OPS + b] = total[a * per_left : (a + 1) * per_left, b * per_right : (b + 1) * per_right]


def swap(array, axis, pairs):
    return lax.ppermute(array, axis, pairs)


def on_device(left, right, bond_signs, hop):
    count, rows, cols = right.shape
    wide, narrow = lax.axis_size("wide"), lax.axis_size("narrow")
    group = LANES // TAPS
    blocks = 2 * (count // group) + 1
    edge_rows = 2 * count + len(EVEN) * TAPS
    parity = (lax.axis_index("wide") % 2).astype(jnp.int32).reshape(1)
    smem = pl.BlockSpec(memory_space=pltpu.SMEM)
    vmem = pl.BlockSpec(memory_space=pltpu.VMEM)

    near, far, side = pl.pallas_call(
        pack_kernel,
        out_shape=(
            jax.ShapeDtypeStruct((RANGE, edge_rows, cols), BF16),
            jax.ShapeDtypeStruct((RANGE, edge_rows, cols), BF16),
            jax.ShapeDtypeStruct((blocks, rows, cols), BF16),
        ),
        in_specs=[smem, vmem, vmem, vmem],
        out_specs=(vmem, vmem, vmem),
        scratch_shapes=[VMEM((edge_rows * SUB, cols), F32), VMEM((edge_rows * SUB, cols), F32)],
        name="pack",
    )(parity, right, left, bond_signs)

    far = swap(far, "wide", [(i, (i + 1) % wide if i % 2 else (i - 1) % wide) for i in range(wide)])
    near = swap(near, "wide", [(i, i ^ 1) for i in range(wide)])
    if narrow == 2:
        side = swap(side, "narrow", [(0, 1), (1, 0)])
    else:
        before = swap(side, "narrow", [(i, (i + 1) % narrow) for i in range(narrow)])
        after = swap(side, "narrow", [((i + 1) % narrow, i) for i in range(narrow)])
        side = jnp.where(lane_index(side.shape) % TAPS < RANGE, before, after)

    per_left, per_right = count // wide, count // narrow
    size = OPS * count
    direct = (OPS * per_right) % LANES == 0 and (OPS * per_left) % 16 == 0
    blocked = (wide * narrow, OPS * per_left, OPS * per_right)
    partial = pl.pallas_call(
        lambda *refs: main_kernel((wide, narrow), *refs),
        out_shape=jax.ShapeDtypeStruct(blocked if direct else (size, size), BF16),
        in_specs=[smem, smem] + [vmem] * 6,
        out_specs=vmem,
        scratch_shapes=[
            VMEM((2, count * (rows + 2 * SUB + 1) + SUB, cols), F32),
            VMEM((2, len(ODD), count * (rows + 1) + SUB, cols), F32),
            VMEM((OPS * TAPS, rows + 2 * SUB, cols), F32),
            VMEM((blocks - 1, len(ODD), rows, cols), F32),
            VMEM((4, 2 * cols, len(ODD) * cols), BF16),
            VMEM((size, size), F32),
        ] + [VMEM((size, 2 * cols), BF16)] * 4,
        name="moments",
    )(parity, hop, right, left, bond_signs, near, far, side)
    if not direct:
        partial = partial.reshape(wide, OPS * per_left, narrow, OPS * per_right).transpose(0, 2, 1, 3).reshape(blocked)
    got = lax.all_to_all(partial, ("wide", "narrow"), 0, 0, tiled=True)
    factor = 1.0 / math.sqrt(rows * cols * wide * narrow)
    return pl.pallas_call(
        lambda *refs: sum_kernel(factor, *refs),
        out_shape=jax.ShapeDtypeStruct((OPS * OPS, per_left, per_right), F32),
        in_specs=[vmem],
        out_specs=vmem,
        name="total",
    )(got)


def solution(mesh):
    in_specs = (
        P(None, "wide", "narrow"),
        P(None, "wide", "narrow"),
        P(None, None, "wide", "narrow"),
        P(),
    )
    out_specs = P(None, "wide", "narrow")
    return jax.shard_map(
        on_device, mesh=mesh, in_specs=in_specs, out_specs=out_specs, check_vma=False
    )
```

```python
import math

import jax
import jax.numpy as jnp
from jax import lax
from jax.experimental import pallas as pl
from jax.experimental.pallas import tpu as pltpu
from jax.sharding import PartitionSpec as P

OPS = 4
RANGE = 4
TAPS = 2 * RANGE
EVEN = tuple(a for a in range(OPS) if a % 2 == 0)
ODD = tuple(a for a in range(OPS) if a % 2 == 1)
SUB = 8
LANES = 128
VMEM = pltpu.VMEM
F32 = jnp.float32
BF16 = jnp.bfloat16
VMEM_LIMIT = 24 * 1024 * 1024


def lane_index(shape):
    return lax.broadcasted_iota(jnp.int32, shape, len(shape) - 1)


def rows_kernel(parity, right, left, bonds, near, far, head, tail):
    count, rows, cols = right.shape
    even = parity[0] == 0

    slot = 0
    for ref, n in ((right, count), (left, count)):
        @pl.loop(0, n)
        def _(v, ref=ref, slot=slot):
            at = pl.multiple_of((v + slot) * SUB, SUB)
            head[pl.ds(at, SUB), :] = ref[v, : 2 * SUB, :].astype(F32)[:SUB]
            tail[pl.ds(at, SUB), :] = ref[v, rows - 2 * SUB :, :].astype(F32)[SUB:]

        slot += n
    for a in EVEN:
        for index in range(TAPS):
            head[slot * SUB : slot * SUB + SUB, :] = (2 * bonds[a, index, :SUB, :] - 1).astype(F32)
            tail[slot * SUB : slot * SUB + SUB, :] = (2 * bonds[a, index, rows - SUB :, :] - 1).astype(F32)
            slot += 1
    for base in range(0, slot, 2 * SUB):
        for row in range(RANGE):
            def strip(ref, offset):
                parts = [ref[pl.ds((base + half * SUB) * SUB + offset, SUB, stride=SUB), :] for half in range(2)]
                return jnp.concatenate(parts, axis=0)

            low = strip(head, row)
            high = strip(tail, SUB - RANGE + row)
            near[row, base : base + 2 * SUB, :] = jnp.where(even, high, low).astype(BF16)
            far[row, base : base + 2 * SUB, :] = jnp.where(even, low, high).astype(BF16)


def sides_kernel(right, left, bonds, side, own, flat):
    count, rows, cols = right.shape
    group = LANES // TAPS
    pitch = rows + 1
    signs = len(ODD) * TAPS

    for which, ref in enumerate((right, left)):
        @pl.loop(0, count, unroll=4)
        def _(v, which=which, ref=ref):
            flat[pl.ds((v + which * count) * pitch, rows), :] = ref[v].astype(F32)

    for t in range(signs):
        at = (2 * count + t) * pitch
        flat[at : at + rows, :] = (2 * bonds[ODD[t // TAPS], t % TAPS] - 1).astype(F32)

    lane = lane_index((2 * SUB, cols)) // TAPS

    @pl.loop(0, (2 * count + signs) // (2 * SUB))
    def _(pair):
        at = pl.multiple_of(pair * 2 * SUB, 2 * SUB)
        for tile in range(rows // group):
            total = jnp.zeros((2 * SUB, cols), F32)
            for r in range(group):
                row = tile * group + r
                strip = jnp.concatenate(
                    [flat[pl.ds((at + half * SUB) * pitch + row, SUB, stride=pitch), :] for half in range(2)], axis=0
                )
                total = jnp.where(lane == r, pltpu.roll(strip, (RANGE + TAPS * r) % LANES, 1), total)
            side[tile, pl.ds(at, 2 * SUB), :] = total.astype(BF16)

    own[...] = side[:, 2 * count :, :]


def main_kernel(widths, parity, hop, right, left, bonds, near, far, side, own, out,
                value, coef, band, mats, matsl, acc, back_a, first_a, back_b, first_b):
    count, rows, cols = right.shape
    even = parity[0] == 0
    group = LANES // TAPS
    stride = rows + 2 * SUB + 1
    period = 2 * TAPS

    def scale_of(a, index):
        return hop[a, index % RANGE] * (1.0 if index < RANGE else -1.0)

    def outer(slab, row):
        low = jnp.where(even, far[row, slab, :].astype(F32), near[row, slab, :].astype(F32))
        high = jnp.where(even, near[row, slab, :].astype(F32), far[row, slab, :].astype(F32))
        return low, high

    for a in range(OPS):
        for index in range(TAPS):
            coef[a * TAPS + index, SUB : SUB + rows, :] = (2 * bonds[a, index] - 1).astype(F32) * scale_of(a, index)
    for row in range(RANGE):
        low, high = outer(slice(2 * count, 2 * count + 2 * SUB), row)
        for slot in range(len(EVEN) * TAPS):
            a, index = EVEN[slot // TAPS], slot % TAPS
            where = SUB - RANGE + row if index < RANGE else SUB + rows + row
            source = low if index < RANGE else high
            coef[a * TAPS + index, where : where + 1, :] = source[slot : slot + 1] * scale_of(a, index)

    tile_shape = (count, cols)
    spot = lane_index((1, cols)) % TAPS
    spots = lane_index(tile_shape) % TAPS
    for tile in range(rows // group):
        mine = own[tile].astype(F32)
        theirs = side[tile, 2 * count :, :].astype(F32)
        for which in range(2):
            packed = side[tile, which * count : (which + 1) * count, :].astype(F32)
            total = {}
            for k in range(1, RANGE + 1):
                moved = jnp.where(spots < RANGE, pltpu.roll(packed, LANES - k, 1), pltpu.roll(packed, k, 1))
                for a in ODD:
                    slot = ODD.index(a) * TAPS + k - 1
                    if which == 0:
                        tops, bottoms = mine[slot : slot + 1], mine[slot + RANGE : slot + RANGE + 1]
                        weight = jnp.where(spot < RANGE, tops * scale_of(a, k - 1), bottoms * scale_of(a, RANGE + k - 1))
                    else:
                        tops = pltpu.roll(theirs, LANES - k, 1)[slot + RANGE : slot + RANGE + 1]
                        bottoms = pltpu.roll(theirs, k, 1)[slot : slot + 1]
                        weight = jnp.where(spot < RANGE, tops * scale_of(a, RANGE + k - 1), bottoms * scale_of(a, k - 1))
                    valid = ((spot < RANGE) & (spot + k >= RANGE)) | ((spot >= RANGE) & (spot - k < RANGE))
                    term = jnp.where(valid, weight, 0.0) * moved
                    total[a] = term if k == 1 else total[a] + term
            for a in ODD:
                band[which, ODD.index(a), tile] = total[a]

    for which, ref in enumerate((right, left)):
        @pl.loop(0, count, unroll=4)
        def _(v, which=which, ref=ref):
            value[which, pl.ds(v * stride + SUB, rows), :] = ref[v].astype(F32)

        for base in range(0, count, 2 * SUB):
            for row in range(RANGE):
                low, high = outer(slice(which * count + base, which * count + base + 2 * SUB), row)
                for half in range(2):
                    at = (base + half * SUB) * stride + row
                    part = slice(half * SUB, half * SUB + SUB)
                    value[which, pl.ds(at + SUB - RANGE, SUB, stride=stride), :] = low[part]
                    value[which, pl.ds(at + SUB + rows, SUB, stride=stride), :] = high[part]

    acc[...] = jnp.zeros_like(acc)

    tile = (period, cols)
    gap = (lane_index(tile) - lax.broadcasted_iota(jnp.int32, tile, 0)) % period
    near_diagonal = lane_index((cols, cols)) - lax.broadcasted_iota(jnp.int32, (cols, cols), 0)
    within = jnp.where((near_diagonal >= -TAPS) & (near_diagonal < TAPS), 1.0, 0.0).astype(BF16)

    def matrices(row, slot):
        for a in ODD:
            total = jnp.zeros(tile, F32)
            for k in range(1, RANGE + 1):
                total = jnp.where(gap == period - k, coef[a * TAPS + k - 1, pl.ds(row + SUB, period, stride=0), :], total)
                total = jnp.where(gap == k, coef[a * TAPS + RANGE + k - 1, pl.ds(row + SUB, period, stride=0), :], total)
            high = total.astype(BF16)
            low = (total - high.astype(F32)).astype(BF16)
            o = ODD.index(a)
            for part, piece in enumerate((high, low)):
                block = jnp.concatenate([piece] * (cols // period), axis=0) * within
                mats[slot, part * cols : (part + 1) * cols, o * cols : (o + 1) * cols] = block
                matsl[slot, o * cols : (o + 1) * cols, part * cols : (part + 1) * cols] = block

    rim_lane = (lane_index(tile_shape) < RANGE) | (lane_index(tile_shape) >= cols - RANGE)

    def stencil(row, part, slot, back, first):
        matrices(row, slot)
        here_lanes = slice(part * cols, (part + 1) * cols)
        tile = row // group
        turn = (2 * LANES - RANGE - TAPS * (row % group)) % LANES
        for which, target in ((0, first), (1, back)):
            middle = jnp.concatenate(
                [value[which, pl.ds(g * SUB * stride + row + SUB, SUB, stride=stride), :] for g in range(count // SUB)], axis=0
            ).astype(BF16)
            middle = jnp.concatenate([middle, middle], axis=1)
            dims = (((1,), (which,)), ((), ()))
            both = lax.dot_general(middle, (mats, matsl)[which][slot], dims, preferred_element_type=F32)
            for o, a in enumerate(ODD):
                beyond = jnp.where(rim_lane, pltpu.roll(band[which, o, tile], turn, 1), 0.0)
                target[a * count : (a + 1) * count, here_lanes] = (both[:, o * cols : (o + 1) * cols] + beyond).astype(BF16)
            factors = {}
            for a in EVEN:
                for index in range(TAPS):
                    step = index % RANGE + 1
                    at = row + SUB if which == 0 else row + SUB + (-step if index < RANGE else step)
                    factors[a, index] = coef[a * TAPS + index, pl.ds(at, SUB, stride=0), :]
            ahead = 1 if which == 0 else -1
            for pair in range(count // (2 * SUB)):
                sums = {a: [] for a in EVEN}
                for half in range(2):
                    here = (2 * pair + half) * SUB * stride + row + SUB
                    total = {}
                    for index in range(TAPS):
                        step = (index % RANGE + 1) * (ahead if index < RANGE else -ahead)
                        moved = value[which, pl.ds(here + step, SUB, stride=stride), :]
                        for a in EVEN:
                            term = factors[a, index] * moved
                            total[a] = term if index == 0 else total[a] + term
                    for a in EVEN:
                        sums[a].append(total[a])
                for a in EVEN:
                    at = a * count + pair * 2 * SUB
                    target[at : at + 2 * SUB, here_lanes] = jnp.concatenate(sums[a], axis=0).astype(BF16)

    def product(back, first):
        acc[...] += lax.dot_general(back[...], first[...], (((1,), (1,)), ((), ())), preferred_element_type=F32)

    back_b[...] = jnp.zeros_like(back_b)
    first_b[...] = jnp.zeros_like(first_b)

    @pl.loop(0, rows // 4)
    def _(step):
        product(back_b, first_b)
        for part in range(2):
            stencil(step * 4 + part, part, part, back_a, first_a)
        product(back_a, first_a)
        for part in range(2):
            stencil(step * 4 + 2 + part, part, 2 + part, back_b, first_b)

    product(back_b, first_b)

    parts_left, parts_right = widths
    per_left, per_right = count // parts_left, count // parts_right
    size = OPS * count

    def order(parts, per, dim):
        new = lax.broadcasted_iota(jnp.int32, (size, size), dim)
        old = lax.broadcasted_iota(jnp.int32, (size, size), 1 - dim)
        part, rest = new // (OPS * per), new % (OPS * per)
        return jnp.where(old == (rest // per) * count + part * per + rest % per, 1.0, 0.0).astype(BF16)

    moved = jnp.dot(order(parts_left, per_left, 0), acc[...].astype(BF16), preferred_element_type=F32).astype(BF16)
    moved = jnp.dot(moved, order(parts_right, per_right, 1), preferred_element_type=F32).astype(BF16)
    if out.ndim == 2:
        out[...] = moved
    else:
        width = OPS * per_right
        for d in range(parts_left * parts_right):
            w, r = divmod(d, parts_right)
            out[d] = moved[w * OPS * per_left : (w + 1) * OPS * per_left, r * width : (r + 1) * width]


def sum_kernel(factor, got, out):
    total = jnp.sum(got[...].astype(F32), axis=0) * factor
    per_left, per_right = out.shape[1], out.shape[2]
    for a in range(OPS):
        for b in range(OPS):
            out[a * OPS + b] = total[a * per_left : (a + 1) * per_left, b * per_right : (b + 1) * per_right]


def swap(array, axis, pairs):
    return lax.ppermute(array, axis, pairs)


def on_device(left, right, bond_signs, hop):
    count, rows, cols = right.shape
    wide, narrow = lax.axis_size("wide"), lax.axis_size("narrow")
    edge_rows = 2 * count + len(EVEN) * TAPS
    side_rows = 2 * count + len(ODD) * TAPS
    tiles = rows * TAPS // LANES
    parity = (lax.axis_index("wide") % 2).astype(jnp.int32).reshape(1)
    smem = pl.BlockSpec(memory_space=pltpu.SMEM)
    vmem = pl.BlockSpec(memory_space=pltpu.VMEM)
    params = pltpu.CompilerParams(vmem_limit_bytes=VMEM_LIMIT)

    near, far = pl.pallas_call(
        rows_kernel,
        out_shape=(jax.ShapeDtypeStruct((RANGE, edge_rows, cols), BF16),) * 2,
        in_specs=[smem, vmem, vmem, vmem],
        out_specs=(vmem, vmem),
        scratch_shapes=[VMEM((edge_rows * SUB, cols), F32), VMEM((edge_rows * SUB, cols), F32)],
        compiler_params=params,
        name="edge_rows",
    )(parity, right, left, bond_signs)
    side, own = pl.pallas_call(
        sides_kernel,
        out_shape=(
            jax.ShapeDtypeStruct((tiles, side_rows, cols), BF16),
            jax.ShapeDtypeStruct((tiles, side_rows - 2 * count, cols), BF16),
        ),
        in_specs=[vmem, vmem, vmem],
        out_specs=(vmem, vmem),
        scratch_shapes=[VMEM((side_rows * (rows + 1) + SUB, cols), F32)],
        compiler_params=params,
        name="edge_columns",
    )(right, left, bond_signs)

    far = swap(far, "wide", [(i, (i + 1) % wide if i % 2 else (i - 1) % wide) for i in range(wide)])
    near = swap(near, "wide", [(i, i ^ 1) for i in range(wide)])
    if narrow == 2:
        side = swap(side, "narrow", [(0, 1), (1, 0)])
    else:
        before = swap(side, "narrow", [(i, (i + 1) % narrow) for i in range(narrow)])
        after = swap(side, "narrow", [((i + 1) % narrow, i) for i in range(narrow)])
        side = jnp.where(lane_index(side.shape) % TAPS < RANGE, before, after)

    per_left, per_right = count // wide, count // narrow
    size = OPS * count
    direct = (OPS * per_right) % LANES == 0 and (OPS * per_left) % 16 == 0
    blocked = (wide * narrow, OPS * per_left, OPS * per_right)
    partial = pl.pallas_call(
        lambda *refs: main_kernel((wide, narrow), *refs),
        out_shape=jax.ShapeDtypeStruct(blocked if direct else (size, size), BF16),
        in_specs=[smem, smem] + [vmem] * 7,
        out_specs=vmem,
        scratch_shapes=[
            VMEM((2, count * (rows + 2 * SUB + 1) + SUB, cols), F32),
            VMEM((OPS * TAPS, rows + 2 * SUB, cols), F32),
            VMEM((2, len(ODD), tiles, count, cols), F32),
            VMEM((4, 2 * cols, len(ODD) * cols), BF16),
            VMEM((4, len(ODD) * cols, 2 * cols), BF16),
            VMEM((size, size), F32),
        ] + [VMEM((size, 2 * cols), BF16)] * 4,
        compiler_params=params,
        name="moments",
    )(parity, hop, right, left, bond_signs, near, far, side, own)
    if not direct:
        partial = partial.reshape(wide, OPS * per_left, narrow, OPS * per_right).transpose(0, 2, 1, 3).reshape(blocked)
    got = lax.all_to_all(partial, ("wide", "narrow"), 0, 0, tiled=True)
    factor = 1.0 / math.sqrt(rows * cols * wide * narrow)
    return pl.pallas_call(
        lambda *refs: sum_kernel(factor, *refs),
        out_shape=jax.ShapeDtypeStruct((OPS * OPS, per_left, per_right), F32),
        in_specs=[vmem],
        out_specs=vmem,
        name="total",
    )(got)


def solution(mesh):
    in_specs = (
        P(None, "wide", "narrow"),
        P(None, "wide", "narrow"),
        P(None, None, "wide", "narrow"),
        P(),
    )
    out_specs = P(None, "wide", "narrow")
    return jax.shard_map(
        on_device, mesh=mesh, in_specs=in_specs, out_specs=out_specs, check_vma=False
    )
```

```python
import math

import jax
import jax.numpy as jnp
from jax import lax
from jax.experimental import pallas as pl
from jax.experimental.pallas import tpu as pltpu
from jax.sharding import PartitionSpec as P


OPS = 4
RANGE = 4
TAPS = 2 * RANGE
EVEN = tuple(a for a in range(OPS) if a % 2 == 0)
ODD = tuple(a for a in range(OPS) if a % 2 == 1)
SUB = 8
LANES = 128
VMEM = pltpu.VMEM
F32 = jnp.float32
BF16 = jnp.bfloat16
VMEM_LIMIT = 24 * 1024 * 1024


def lane_index(shape):
    return lax.broadcasted_iota(jnp.int32, shape, len(shape) - 1)


def rows_kernel(parity, right, left, bonds, near, far, head, tail, ends, signs, sems):
    count, rows, _ = right.shape
    even = parity[0] == 0

    copies = []
    for end, at in enumerate((0, rows - 2 * SUB)):
        for which, ref in enumerate((right, left)):
            copies.append((ref.at[:, pl.ds(at, 2 * SUB), :], ends.at[end, which]))
    for end, at in enumerate((0, rows - SUB)):
        for o, a in enumerate(EVEN):
            copies.append((bonds.at[a, :, pl.ds(at, SUB), :], signs.at[end, o]))
    copies = [pltpu.make_async_copy(src, dst, sems.at[n]) for n, (src, dst) in enumerate(copies)]
    for copy in copies:
        copy.start()
    for copy in copies:
        copy.wait()

    slot = 0
    for which in range(2):
        @pl.loop(0, count, unroll=4)
        def _(v, which=which, slot=slot):
            at = pl.multiple_of((v + slot) * SUB, SUB)
            head[pl.ds(at, SUB), :] = ends[0, which, v].astype(F32)[:SUB]
            tail[pl.ds(at, SUB), :] = ends[1, which, v].astype(F32)[SUB:]

        slot += count
    for o in range(len(EVEN)):
        for index in range(TAPS):
            head[slot * SUB : slot * SUB + SUB, :] = (2 * signs[0, o, index] - 1).astype(F32)
            tail[slot * SUB : slot * SUB + SUB, :] = (2 * signs[1, o, index] - 1).astype(F32)
            slot += 1
    for base in range(0, slot, 2 * SUB):
        for row in range(RANGE):
            def strip(ref, offset):
                parts = [ref[pl.ds((base + half * SUB) * SUB + offset, SUB, stride=SUB), :] for half in range(2)]
                return jnp.concatenate(parts, axis=0)

            low = strip(head, row)
            high = strip(tail, SUB - RANGE + row)
            near[row, base : base + 2 * SUB, :] = jnp.where(even, high, low).astype(BF16)
            far[row, base : base + 2 * SUB, :] = jnp.where(even, low, high).astype(BF16)


def sides_kernel(right, left, bonds, side, own, flat):
    count, rows, cols = right.shape
    group = LANES // TAPS
    pitch = rows + 1
    signs = len(ODD) * TAPS

    for which, ref in enumerate((right, left)):
        @pl.loop(0, count, unroll=4)
        def _(v, which=which, ref=ref):
            flat[pl.ds((v + which * count) * pitch, rows), :] = ref[v].astype(F32)

    for t in range(signs):
        at = (2 * count + t) * pitch
        flat[at : at + rows, :] = (2 * bonds[ODD[t // TAPS], t % TAPS] - 1).astype(F32)

    lane = lane_index((2 * SUB, cols)) // TAPS

    @pl.loop(0, (2 * count + signs) // (2 * SUB))
    def _(pair):
        at = pl.multiple_of(pair * 2 * SUB, 2 * SUB)
        for tile in range(rows // group):
            total = jnp.zeros((2 * SUB, cols), F32)
            for r in range(group):
                row = tile * group + r
                strip = jnp.concatenate(
                    [flat[pl.ds((at + half * SUB) * pitch + row, SUB, stride=pitch), :] for half in range(2)], axis=0
                )
                total = jnp.where(lane == r, pltpu.roll(strip, (RANGE + TAPS * r) % LANES, 1), total)
            side[tile, pl.ds(at, 2 * SUB), :] = total.astype(BF16)

    own[...] = side[:, 2 * count :, :]


def main_kernel(widths, parity, hop, right, left, bonds, near, far, side, own, out,
                value, coef, band, acc):
    count, rows, cols = right.shape
    even = parity[0] == 0
    group = LANES // TAPS
    stride = rows + 2 * SUB + 1
    period = 2 * TAPS

    def scale_of(a, index):
        return hop[a, index % RANGE] * (1.0 if index < RANGE else -1.0)

    def outer(slab, row):
        low = jnp.where(even, far[row, slab, :].astype(F32), near[row, slab, :].astype(F32))
        high = jnp.where(even, near[row, slab, :].astype(F32), far[row, slab, :].astype(F32))
        return low, high

    for a in range(OPS):
        for index in range(TAPS):
            coef[a * TAPS + index, SUB : SUB + rows, :] = (2 * bonds[a, index] - 1).astype(F32) * scale_of(a, index)
    for row in range(RANGE):
        low, high = outer(slice(2 * count, 2 * count + 2 * SUB), row)
        for slot in range(len(EVEN) * TAPS):
            a, index = EVEN[slot // TAPS], slot % TAPS
            where = SUB - RANGE + row if index < RANGE else SUB + rows + row
            source = low if index < RANGE else high
            coef[a * TAPS + index, where : where + 1, :] = source[slot : slot + 1] * scale_of(a, index)

    tile_shape = (count, cols)
    spot = lane_index((1, cols)) % TAPS
    spots = lane_index(tile_shape) % TAPS
    for tile in range(rows // group):
        mine = own[tile].astype(F32)
        theirs = side[tile, 2 * count :, :].astype(F32)
        for which in range(2):
            packed = side[tile, which * count : (which + 1) * count, :].astype(F32)
            total = {}
            for k in range(1, RANGE + 1):
                moved = jnp.where(spots < RANGE, pltpu.roll(packed, LANES - k, 1), pltpu.roll(packed, k, 1))
                for a in ODD:
                    slot = ODD.index(a) * TAPS + k - 1
                    if which == 0:
                        tops, bottoms = mine[slot : slot + 1], mine[slot + RANGE : slot + RANGE + 1]
                        weight = jnp.where(spot < RANGE, tops * scale_of(a, k - 1), bottoms * scale_of(a, RANGE + k - 1))
                    else:
                        tops = pltpu.roll(theirs, LANES - k, 1)[slot + RANGE : slot + RANGE + 1]
                        bottoms = pltpu.roll(theirs, k, 1)[slot : slot + 1]
                        weight = jnp.where(spot < RANGE, tops * scale_of(a, RANGE + k - 1), bottoms * scale_of(a, k - 1))
                    valid = ((spot < RANGE) & (spot + k >= RANGE)) | ((spot >= RANGE) & (spot - k < RANGE))
                    term = jnp.where(valid, weight, 0.0) * moved
                    total[a] = term if k == 1 else total[a] + term
            for a in ODD:
                band[which, ODD.index(a), tile] = total[a]

    for which, ref in enumerate((right, left)):
        @pl.loop(0, count, unroll=4)
        def _(v, which=which, ref=ref):
            value[which, pl.ds(v * stride + SUB, rows), :] = ref[v].astype(F32)

        for base in range(0, count, 2 * SUB):
            for row in range(RANGE):
                low, high = outer(slice(which * count + base, which * count + base + 2 * SUB), row)
                for half in range(2):
                    at = (base + half * SUB) * stride + row
                    part = slice(half * SUB, half * SUB + SUB)
                    value[which, pl.ds(at + SUB - RANGE, SUB, stride=stride), :] = low[part]
                    value[which, pl.ds(at + SUB + rows, SUB, stride=stride), :] = high[part]

    acc[...] = jnp.zeros_like(acc)

    tile = (period, cols)
    gap = (lane_index(tile) - lax.broadcasted_iota(jnp.int32, tile, 0)) % period
    near_diagonal = lane_index((cols, cols)) - lax.broadcasted_iota(jnp.int32, (cols, cols), 0)
    within = jnp.where((near_diagonal >= -TAPS) & (near_diagonal < TAPS), 1.0, 0.0).astype(BF16)

    def matrices(row):
        pieces = {}
        for a in ODD:
            total = jnp.zeros(tile, F32)
            for k in range(1, RANGE + 1):
                total = jnp.where(gap == period - k, coef[a * TAPS + k - 1, pl.ds(row + SUB, period, stride=0), :], total)
                total = jnp.where(gap == k, coef[a * TAPS + RANGE + k - 1, pl.ds(row + SUB, period, stride=0), :], total)
            high = total.astype(BF16)
            low = (total - high.astype(F32)).astype(BF16)
            for part, piece in enumerate((high, low)):
                pieces[part, a] = jnp.concatenate([piece] * (cols // period), axis=0) * within
        right_side = jnp.concatenate([jnp.concatenate([pieces[part, a] for a in ODD], axis=1) for part in range(2)], axis=0)
        left_side = jnp.concatenate([jnp.concatenate([pieces[part, a] for part in range(2)], axis=1) for a in ODD], axis=0)
        return right_side, left_side

    rim_lane = (lane_index(tile_shape) < RANGE) | (lane_index(tile_shape) >= cols - RANGE)

    def stencil(row):
        bands = matrices(row)
        results = []
        tile = row // group
        turn = (2 * LANES - RANGE - TAPS * (row % group)) % LANES
        for which in range(2):
            done = {}
            middle = jnp.concatenate(
                [value[which, pl.ds(g * SUB * stride + row + SUB, SUB, stride=stride), :] for g in range(count // SUB)], axis=0
            ).astype(BF16)
            middle = jnp.concatenate([middle, middle], axis=1)
            dims = (((1,), (which,)), ((), ()))
            both = lax.dot_general(middle, bands[which], dims, preferred_element_type=F32)
            for o, a in enumerate(ODD):
                beyond = jnp.where(rim_lane, pltpu.roll(band[which, o, tile], turn, 1), 0.0)
                done[a] = [(both[:, o * cols : (o + 1) * cols] + beyond).astype(BF16)]
            factors = {}
            for a in EVEN:
                for index in range(TAPS):
                    step = index % RANGE + 1
                    at = row + SUB if which == 0 else row + SUB + (-step if index < RANGE else step)
                    factors[a, index] = coef[a * TAPS + index, pl.ds(at, SUB, stride=0), :]
            ahead = 1 if which == 0 else -1
            for pair in range(count // (2 * SUB)):
                sums = {a: [] for a in EVEN}
                for half in range(2):
                    here = (2 * pair + half) * SUB * stride + row + SUB
                    total = {}
                    for index in range(TAPS):
                        step = (index % RANGE + 1) * (ahead if index < RANGE else -ahead)
                        moved = value[which, pl.ds(here + step, SUB, stride=stride), :]
                        for a in EVEN:
                            term = factors[a, index] * moved
                            total[a] = term if index == 0 else total[a] + term
                    for a in EVEN:
                        sums[a].append(total[a])
                for a in EVEN:
                    done.setdefault(a, []).append(jnp.concatenate(sums[a], axis=0).astype(BF16))
            results.append(jnp.concatenate([piece for a in range(OPS) for piece in done[a]], axis=0))
        return results

    @pl.loop(0, rows // 16)
    def _(step):
        for start in range(0, 16, 2):
            found = [stencil(step * 16 + start + n) for n in range(2)]
            first = jnp.concatenate([one[0] for one in found], axis=1)
            back = jnp.concatenate([one[1] for one in found], axis=1)
            acc[...] += lax.dot_general(back, first, (((1,), (1,)), ((), ())), preferred_element_type=F32)

    parts_left, parts_right = widths
    per_left, per_right = count // parts_left, count // parts_right
    size = OPS * count

    def order(per, dim):
        new = lax.broadcasted_iota(jnp.int32, (size, size), dim)
        old = lax.broadcasted_iota(jnp.int32, (size, size), 1 - dim)
        part, rest = new // (OPS * per), new % (OPS * per)
        return jnp.where(old == (rest // per) * count + part * per + rest % per, 1.0, 0.0).astype(BF16)

    moved = jnp.dot(order(per_left, 0), acc[...].astype(BF16), preferred_element_type=F32).astype(BF16)
    moved = jnp.dot(moved, order(per_right, 1), preferred_element_type=F32).astype(BF16)
    if out.ndim == 2:
        out[...] = moved
    else:
        width = OPS * per_right
        for d in range(parts_left * parts_right):
            w, r = divmod(d, parts_right)
            out[d] = moved[w * OPS * per_left : (w + 1) * OPS * per_left, r * width : (r + 1) * width]


def sum_kernel(factor, got, out):
    total = jnp.sum(got[...].astype(F32), axis=0) * factor
    per_left, per_right = out.shape[1], out.shape[2]
    for a in range(OPS):
        for b in range(OPS):
            out[a * OPS + b] = total[a * per_left : (a + 1) * per_left, b * per_right : (b + 1) * per_right]


def swap(array, axis, pairs):
    return lax.ppermute(array, axis, pairs)


def on_device(left, right, bond_signs, hop):
    count, rows, cols = right.shape
    wide, narrow = lax.axis_size("wide"), lax.axis_size("narrow")
    edge_rows = 2 * count + len(EVEN) * TAPS
    side_rows = 2 * count + len(ODD) * TAPS
    tiles = rows * TAPS // LANES
    parity = (lax.axis_index("wide") % 2).astype(jnp.int32).reshape(1)
    smem = pl.BlockSpec(memory_space=pltpu.SMEM)
    vmem = pl.BlockSpec(memory_space=pltpu.VMEM)
    params = pltpu.CompilerParams(vmem_limit_bytes=VMEM_LIMIT)

    hbm = pl.BlockSpec(memory_space=pltpu.HBM)

    near, far = pl.pallas_call(
        rows_kernel,
        out_shape=(jax.ShapeDtypeStruct((RANGE, edge_rows, cols), BF16),) * 2,
        in_specs=[smem, hbm, hbm, hbm],
        out_specs=(vmem, vmem),
        scratch_shapes=[
            VMEM((edge_rows * SUB, cols), F32),
            VMEM((edge_rows * SUB, cols), F32),
            VMEM((2, 2, count, 2 * SUB, cols), BF16),
            VMEM((2, len(EVEN), TAPS, SUB, cols), jnp.int32),
            pltpu.SemaphoreType.DMA((4 + 2 * len(EVEN),)),
        ],
        compiler_params=params,
        name="edge_rows",
    )(parity, right, left, bond_signs)
    side, own = pl.pallas_call(
        sides_kernel,
        out_shape=(
            jax.ShapeDtypeStruct((tiles, side_rows, cols), BF16),
            jax.ShapeDtypeStruct((tiles, side_rows - 2 * count, cols), BF16),
        ),
        in_specs=[vmem, vmem, vmem],
        out_specs=(vmem, vmem),
        scratch_shapes=[VMEM((side_rows * (rows + 1) + SUB, cols), F32)],
        compiler_params=params,
        name="edge_columns",
    )(right, left, bond_signs)

    far = swap(far, "wide", [(i, (i + 1) % wide if i % 2 else (i - 1) % wide) for i in range(wide)])
    near = swap(near, "wide", [(i, i ^ 1) for i in range(wide)])
    if narrow == 2:
        side = swap(side, "narrow", [(0, 1), (1, 0)])
    else:
        before = swap(side, "narrow", [(i, (i + 1) % narrow) for i in range(narrow)])
        after = swap(side, "narrow", [((i + 1) % narrow, i) for i in range(narrow)])
        side = jnp.where(lane_index(side.shape) % TAPS < RANGE, before, after)

    per_left, per_right = count // wide, count // narrow
    size = OPS * count
    direct = (OPS * per_right) % LANES == 0 and (OPS * per_left) % 16 == 0
    blocked = (wide * narrow, OPS * per_left, OPS * per_right)
    partial = pl.pallas_call(
        lambda *refs: main_kernel((wide, narrow), *refs),
        out_shape=jax.ShapeDtypeStruct(blocked if direct else (size, size), BF16),
        in_specs=[smem, smem] + [vmem] * 7,
        out_specs=vmem,
        scratch_shapes=[
            VMEM((2, count * (rows + 2 * SUB + 1) + SUB, cols), F32),
            VMEM((OPS * TAPS, rows + 2 * SUB, cols), F32),
            VMEM((2, len(ODD), tiles, count, cols), F32),
            VMEM((size, size), F32),
        ],
        compiler_params=params,
        name="moments",
    )(parity, hop, right, left, bond_signs, near, far, side, own)
    if not direct:
        partial = partial.reshape(wide, OPS * per_left, narrow, OPS * per_right).transpose(0, 2, 1, 3).reshape(blocked)
    got = lax.all_to_all(partial, ("wide", "narrow"), 0, 0, tiled=True)
    factor = 1.0 / math.sqrt(rows * cols * wide * narrow)
    return pl.pallas_call(
        lambda *refs: sum_kernel(factor, *refs),
        out_shape=jax.ShapeDtypeStruct((OPS * OPS, per_left, per_right), F32),
        in_specs=[vmem],
        out_specs=vmem,
        name="total",
    )(got)


def solution(mesh):
    in_specs = (
        P(None, "wide", "narrow"),
        P(None, "wide", "narrow"),
        P(None, None, "wide", "narrow"),
        P(),
    )
    out_specs = P(None, "wide", "narrow")

    return jax.shard_map(on_device, mesh=mesh, in_specs=in_specs, out_specs=out_specs, check_vma=False)
```

```python
import math

import jax
import jax.numpy as jnp
from jax import lax
from jax.experimental import pallas as pl
from jax.experimental.pallas import tpu as pltpu
from jax.sharding import PartitionSpec as P


OPS = 4
RANGE = 4
TAPS = 2 * RANGE
EVEN = tuple(a for a in range(OPS) if a % 2 == 0)
ODD = tuple(a for a in range(OPS) if a % 2 == 1)
SUB = 8
LANES = 128
VMEM = pltpu.VMEM
F32 = jnp.float32
BF16 = jnp.bfloat16
INNER_BODY = 4
MAIN_BODY = 8
VMEM_LIMIT = 24 * 1024 * 1024


def lane_index(shape):
    return lax.broadcasted_iota(jnp.int32, shape, len(shape) - 1)


def pack_kernel(parity, hop, right, left, bonds, near, far, side, own, value, coef, vectors, bits, flat, head, tail, sems):
    count, rows, cols = right.shape
    even = parity[0] == 0
    group = LANES // TAPS
    pitch = rows + 1
    batch = 2 * SUB
    batches = count // batch

    copies = []
    for which, ref in enumerate((right, left)):
        for n in range(batches):
            copies.append((ref.at[pl.ds(n * batch, batch)], vectors.at[which, pl.ds(n * batch, batch)]))
    for a in ODD + EVEN:
        copies.append((bonds.at[a], bits.at[a]))
    copies = [pltpu.make_async_copy(src, dst, sems.at[n]) for n, (src, dst) in enumerate(copies)]
    for copy in copies:
        copy.start()

    lane = lane_index((batch, cols)) // TAPS

    def pack(at, flat):
        for tile in range(rows // group):
            total = jnp.zeros((batch, cols), F32)
            for r in range(group):
                row = tile * group + r
                strip = jnp.concatenate(
                    [flat[pl.ds(half * SUB * pitch + row, SUB, stride=pitch), :] for half in range(2)], axis=0
                )
                total = jnp.where(lane == r, pltpu.roll(strip, (RANGE + TAPS * r) % LANES, 1), total)
            side[tile, at : at + batch, :] = total.astype(BF16)

    def send(at):
        for row in range(RANGE):
            def strip(ref, offset):
                parts = [ref[pl.ds((at + half * SUB) * SUB + offset, SUB, stride=SUB), :] for half in range(2)]
                return jnp.concatenate(parts, axis=0)

            low = strip(head, row)
            high = strip(tail, SUB - RANGE + row)
            near[row, at : at + batch, :] = jnp.where(even, high, low).astype(BF16)
            far[row, at : at + batch, :] = jnp.where(even, low, high).astype(BF16)

    for which in range(2):
        for n in range(batches):
            copies[which * batches + n].wait()
            at = which * count + n * batch
            for v in range(batch):
                one = vectors[which, n * batch + v].astype(F32)
                start = (n * batch + v) * pitch
                value[which, start : start + rows, :] = one
                head[(at + v) * SUB : (at + v + 1) * SUB, :] = one[:SUB]
                tail[(at + v) * SUB : (at + v + 1) * SUB, :] = one[rows - SUB :]
            pack(at, value.at[which, pl.ds(n * batch * pitch, batch * pitch)])
            send(at)
    at = 2 * count
    for n, a in enumerate(ODD + EVEN):
        copies[2 * batches + n].wait()
        for index in range(TAPS):
            scale = hop[a, index % RANGE] * (1.0 if index < RANGE else -1.0)
            sign = (2 * bits[a, index] - 1).astype(F32)
            coef[a * TAPS + index] = sign * scale
            if a in ODD:
                t = ODD.index(a) * TAPS + index
                flat[t * pitch : t * pitch + rows, :] = sign
            else:
                t = at + EVEN.index(a) * TAPS + index
                head[t * SUB : (t + 1) * SUB, :] = sign[:SUB]
                tail[t * SUB : (t + 1) * SUB, :] = sign[rows - SUB :]
    pack(at, flat)
    send(at)
    own[...] = side[:, at:, :]


def along_rows(which, value_at, factor_at):
    totals = {}
    for index in range(TAPS):
        step = (index % RANGE + 1) * (1 if index < RANGE else -1) * (1 if which == 0 else -1)
        moved = value_at(step)
        for a in EVEN:
            term = factor_at(a, index) * moved
            totals[a] = term if index == 0 else totals[a] + term
    return totals


def factor_row(which, row, index):
    step = index % RANGE + 1
    return row if which == 0 else row + (-step if index < RANGE else step)


def inner_kernel(value, coef, inner, along):
    _, rows, count, _ = along.shape
    cols = coef.shape[2]
    pitch = rows + 1
    period = 2 * TAPS

    tile = (period, cols)
    gap = (lane_index(tile) - lax.broadcasted_iota(jnp.int32, tile, 0)) % period
    near_diagonal = lane_index((cols, cols)) - lax.broadcasted_iota(jnp.int32, (cols, cols), 0)
    within = jnp.where((near_diagonal >= -TAPS) & (near_diagonal < TAPS), 1.0, 0.0).astype(BF16)

    def matrices(row):
        pieces = {}
        for a in ODD:
            total = jnp.zeros(tile, F32)
            for k in range(1, RANGE + 1):
                total = jnp.where(gap == period - k, coef[a * TAPS + k - 1, pl.ds(row, period, stride=0), :], total)
                total = jnp.where(gap == k, coef[a * TAPS + RANGE + k - 1, pl.ds(row, period, stride=0), :], total)
            high = total.astype(BF16)
            low = (total - high.astype(F32)).astype(BF16)
            for part, piece in enumerate((high, low)):
                pieces[part, a] = jnp.concatenate([piece] * (cols // period), axis=0) * within
        right_side = jnp.concatenate([jnp.concatenate([pieces[part, a] for a in ODD], axis=1) for part in range(2)], axis=0)
        left_side = jnp.concatenate([jnp.concatenate([pieces[part, a] for part in range(2)], axis=1) for a in ODD], axis=0)
        return right_side, left_side

    def strip(which, g, row):
        return value[which, pl.ds(g * SUB * pitch + row, SUB, stride=pitch), :]

    def columns(row):
        bands = matrices(row)
        for which in range(2):
            middle = jnp.concatenate([strip(which, g, row) for g in range(count // SUB)], axis=0).astype(BF16)
            middle = jnp.concatenate([middle, middle], axis=1)
            dims = (((1,), (which,)), ((), ()))
            along[which, row] = lax.dot_general(middle, bands[which], dims, preferred_element_type=F32)

    def lines(row):
        for which in range(2):
            factors = {}
            for a in EVEN:
                for index in range(TAPS):
                    factors[a, index] = coef[a * TAPS + index, pl.ds(factor_row(which, row, index), SUB, stride=0), :]
            for pair in range(count // (2 * SUB)):
                halves = [
                    along_rows(which, lambda step, g=2 * pair + half: strip(which, g, row + step), lambda a, index: factors[a, index])
                    for half in range(2)
                ]
                for o, a in enumerate(EVEN):
                    at = o * count + pair * 2 * SUB
                    inner[which, row, at : at + 2 * SUB, :] = jnp.concatenate([half[a] for half in halves], axis=0).astype(BF16)

    @pl.loop(0, RANGE // 2)
    def _(n):
        for one in range(2):
            columns(2 * n + one)
            columns(rows - RANGE + 2 * n + one)

    @pl.loop(0, (rows - 2 * RANGE) // INNER_BODY)
    def _(step):
        for n in range(INNER_BODY):
            row = RANGE + step * INNER_BODY + n
            columns(row)
            lines(row)


def main_kernel(widths, parity, hop, coef, value, inner, along, near, far, side, own, out, band, near_ends, ends, acc):
    _, rows, count, _ = along.shape
    cols = coef.shape[2]
    pitch = rows + 1
    even = parity[0] == 0
    group = LANES // TAPS

    def scale_of(a, index):
        return hop[a, index % RANGE] * (1.0 if index < RANGE else -1.0)

    def outer(slab, row):
        low = jnp.where(even, far[row, slab, :].astype(F32), near[row, slab, :].astype(F32))
        high = jnp.where(even, near[row, slab, :].astype(F32), far[row, slab, :].astype(F32))
        return low, high

    for row in range(RANGE):
        low, high = outer(slice(2 * count, 2 * count + 2 * SUB), row)
        for slot in range(len(EVEN) * TAPS):
            a, index = EVEN[slot // TAPS], slot % TAPS
            source = low if index < RANGE else high
            near_ends[slot, row : row + 1, :] = source[slot : slot + 1] * scale_of(a, index)

    for end in range(2):
        for n in range(RANGE):
            row = n if end == 0 else rows - RANGE + n
            for which in range(2):
                def value_at(step, base):
                    at = row + step
                    slab = slice(which * count + base, which * count + base + 2 * SUB)
                    if at < 0:
                        return outer(slab, at + RANGE)[0]
                    if at >= rows:
                        return outer(slab, at - rows)[1]
                    parts = [value[which, pl.ds((base + half * SUB) * pitch + at, SUB, stride=pitch), :] for half in range(2)]
                    return jnp.concatenate(parts, axis=0)

                def factor_at(a, index):
                    at = factor_row(which, row, index)
                    if 0 <= at < rows:
                        one = coef[a * TAPS + index, at : at + 1, :]
                    else:
                        at = at + RANGE if at < 0 else at - rows
                        one = near_ends[EVEN.index(a) * TAPS + index, at : at + 1, :]
                    return jnp.broadcast_to(one, (2 * SUB, cols))

                for base in range(0, count, 2 * SUB):
                    totals = along_rows(which, lambda step, base=base: value_at(step, base), factor_at)
                    for o, a in enumerate(EVEN):
                        at = o * count + base
                        ends[which, end * RANGE + n, at : at + 2 * SUB, :] = totals[a].astype(BF16)

    tile_shape = (count, cols)
    spot = lane_index((1, cols)) % TAPS
    spots = lane_index(tile_shape) % TAPS
    for tile in range(rows // group):
        mine = own[tile].astype(F32)
        theirs = side[tile, 2 * count :, :].astype(F32)
        for which in range(2):
            packed = side[tile, which * count : (which + 1) * count, :].astype(F32)
            total = {}
            for k in range(1, RANGE + 1):
                moved = jnp.where(spots < RANGE, pltpu.roll(packed, LANES - k, 1), pltpu.roll(packed, k, 1))
                for a in ODD:
                    slot = ODD.index(a) * TAPS + k - 1
                    if which == 0:
                        tops, bottoms = mine[slot : slot + 1], mine[slot + RANGE : slot + RANGE + 1]
                        weight = jnp.where(spot < RANGE, tops * scale_of(a, k - 1), bottoms * scale_of(a, RANGE + k - 1))
                    else:
                        tops = pltpu.roll(theirs, LANES - k, 1)[slot + RANGE : slot + RANGE + 1]
                        bottoms = pltpu.roll(theirs, k, 1)[slot : slot + 1]
                        weight = jnp.where(spot < RANGE, tops * scale_of(a, RANGE + k - 1), bottoms * scale_of(a, k - 1))
                    valid = ((spot < RANGE) & (spot + k >= RANGE)) | ((spot >= RANGE) & (spot - k < RANGE))
                    term = jnp.where(valid, weight, 0.0) * moved
                    total[a] = term if k == 1 else total[a] + term
            for a in ODD:
                band[which, ODD.index(a), tile] = total[a]

    acc[...] = jnp.zeros_like(acc)
    rim_lane = (lane_index(tile_shape) < RANGE) | (lane_index(tile_shape) >= cols - RANGE)

    def results(row, even_of):
        found = []
        tile = row // group
        turn = (2 * LANES - RANGE - TAPS * (row % group)) % LANES
        for which in range(2):
            both = along[which, row]
            done = {a: even_of(which)[EVEN.index(a) * count : (EVEN.index(a) + 1) * count] for a in EVEN}
            for o, a in enumerate(ODD):
                beyond = jnp.where(rim_lane, pltpu.roll(band[which, o, tile], turn, 1), 0.0)
                done[a] = (both[:, o * cols : (o + 1) * cols] + beyond).astype(BF16)
            found.append(jnp.concatenate([done[a] for a in range(OPS)], axis=0))
        return found

    def accumulate(pairs):
        for pair in pairs:
            found = [results(*one) for one in pair]
            first = jnp.concatenate([one[0] for one in found], axis=1)
            back = jnp.concatenate([one[1] for one in found], axis=1)
            acc[...] += lax.dot_general(back, first, (((1,), (1,)), ((), ())), preferred_element_type=F32)

    def end_row(n):
        return (n if n < RANGE else rows - 2 * RANGE + n), lambda which: ends[which, n]

    accumulate([[end_row(n), end_row(n + 1)] for n in range(0, 2 * RANGE, 2)])

    @pl.loop(0, (rows - 2 * RANGE) // MAIN_BODY)
    def _(step):
        def inner_row(n):
            row = RANGE + step * MAIN_BODY + n
            return row, lambda which: inner[which, row]

        accumulate([[inner_row(n), inner_row(n + 1)] for n in range(0, MAIN_BODY, 2)])

    parts_left, parts_right = widths
    per_left, per_right = count // parts_left, count // parts_right
    size = OPS * count

    def order(per, dim):
        new = lax.broadcasted_iota(jnp.int32, (size, size), dim)
        old = lax.broadcasted_iota(jnp.int32, (size, size), 1 - dim)
        part, rest = new // (OPS * per), new % (OPS * per)
        return jnp.where(old == (rest // per) * count + part * per + rest % per, 1.0, 0.0).astype(BF16)

    moved = jnp.dot(order(per_left, 0), acc[...].astype(BF16), preferred_element_type=F32).astype(BF16)
    moved = jnp.dot(moved, order(per_right, 1), preferred_element_type=F32).astype(BF16)
    if out.ndim == 2:
        out[...] = moved
    else:
        width = OPS * per_right
        for d in range(parts_left * parts_right):
            w, r = divmod(d, parts_right)
            out[d] = moved[w * OPS * per_left : (w + 1) * OPS * per_left, r * width : (r + 1) * width]


def sum_kernel(factor, got, out):
    total = jnp.sum(got[...].astype(F32), axis=0) * factor
    per_left, per_right = out.shape[1], out.shape[2]
    for a in range(OPS):
        for b in range(OPS):
            out[a * OPS + b] = total[a * per_left : (a + 1) * per_left, b * per_right : (b + 1) * per_right]


def swap(array, axis, pairs):
    return lax.ppermute(array, axis, pairs)


def on_device(left, right, bond_signs, hop):
    count, rows, cols = right.shape
    wide, narrow = lax.axis_size("wide"), lax.axis_size("narrow")
    edge_rows = 2 * count + len(EVEN) * TAPS
    side_rows = 2 * count + len(ODD) * TAPS
    tiles = rows * TAPS // LANES
    parity = (lax.axis_index("wide") % 2).astype(jnp.int32).reshape(1)
    smem = pl.BlockSpec(memory_space=pltpu.SMEM)
    vmem = pl.BlockSpec(memory_space=pltpu.VMEM)
    params = pltpu.CompilerParams(vmem_limit_bytes=VMEM_LIMIT)

    hbm = pl.BlockSpec(memory_space=pltpu.HBM)

    near, far, side, own, value, coef = pl.pallas_call(
        pack_kernel,
        out_shape=(
            jax.ShapeDtypeStruct((RANGE, edge_rows, cols), BF16),
            jax.ShapeDtypeStruct((RANGE, edge_rows, cols), BF16),
            jax.ShapeDtypeStruct((tiles, side_rows, cols), BF16),
            jax.ShapeDtypeStruct((tiles, side_rows - 2 * count, cols), BF16),
            jax.ShapeDtypeStruct((2, count * (rows + 1), cols), F32),
            jax.ShapeDtypeStruct((OPS * TAPS, rows, cols), F32),
        ),
        in_specs=[smem, smem, hbm, hbm, hbm],
        out_specs=(vmem,) * 6,
        scratch_shapes=[
            VMEM((2, count, rows, cols), BF16),
            VMEM((OPS, TAPS, rows, cols), jnp.int32),
            VMEM((2 * SUB * (rows + 1), cols), F32),
            VMEM((edge_rows * SUB, cols), F32),
            VMEM((edge_rows * SUB, cols), F32),
            pltpu.SemaphoreType.DMA((2 * (count // (2 * SUB)) + OPS,)),
        ],
        compiler_params=params,
        name="pack",
    )(parity, hop, *(pltpu.with_memory_space_constraint(one, pltpu.HBM) for one in (right, left, bond_signs)))
    inner, along = pl.pallas_call(
        inner_kernel,
        out_shape=(
            jax.ShapeDtypeStruct((2, rows, len(EVEN) * count, cols), BF16),
            jax.ShapeDtypeStruct((2, rows, count, len(ODD) * cols), F32),
        ),
        in_specs=[vmem, vmem],
        out_specs=(vmem,) * 2,
        compiler_params=params,
        name="interior",
    )(value, coef)

    far = swap(far, "wide", [(i, (i + 1) % wide if i % 2 else (i - 1) % wide) for i in range(wide)])
    near = swap(near, "wide", [(i, i ^ 1) for i in range(wide)])
    if narrow == 2:
        side = swap(side, "narrow", [(0, 1), (1, 0)])
    else:
        before = swap(side, "narrow", [(i, (i + 1) % narrow) for i in range(narrow)])
        after = swap(side, "narrow", [((i + 1) % narrow, i) for i in range(narrow)])
        side = jnp.where(lane_index(side.shape) % TAPS < RANGE, before, after)

    per_left, per_right = count // wide, count // narrow
    size = OPS * count
    direct = (OPS * per_right) % LANES == 0 and (OPS * per_left) % 16 == 0
    blocked = (wide * narrow, OPS * per_left, OPS * per_right)
    partial = pl.pallas_call(
        lambda *refs: main_kernel((wide, narrow), *refs),
        out_shape=jax.ShapeDtypeStruct(blocked if direct else (size, size), BF16),
        in_specs=[smem, smem] + [vmem] * 8,
        out_specs=vmem,
        scratch_shapes=[
            VMEM((2, len(ODD), tiles, count, cols), F32),
            VMEM((len(EVEN) * TAPS, RANGE, cols), F32),
            VMEM((2, 2 * RANGE, len(EVEN) * count, cols), BF16),
            VMEM((size, size), F32),
        ],
        compiler_params=params,
        name="moments",
    )(parity, hop, coef, value, inner, along, near, far, side, own)
    if not direct:
        partial = partial.reshape(wide, OPS * per_left, narrow, OPS * per_right).transpose(0, 2, 1, 3).reshape(blocked)
    got = lax.all_to_all(partial, ("wide", "narrow"), 0, 0, tiled=True)
    factor = 1.0 / math.sqrt(rows * cols * wide * narrow)
    return pl.pallas_call(
        lambda *refs: sum_kernel(factor, *refs),
        out_shape=jax.ShapeDtypeStruct((OPS * OPS, per_left, per_right), F32),
        in_specs=[vmem],
        out_specs=vmem,
        name="total",
    )(got)


def solution(mesh):
    in_specs = (
        P(None, "wide", "narrow"),
        P(None, "wide", "narrow"),
        P(None, None, "wide", "narrow"),
        P(),
    )
    out_specs = P(None, "wide", "narrow")

    return jax.shard_map(on_device, mesh=mesh, in_specs=in_specs, out_specs=out_specs, check_vma=False)
```

```python
import math

import jax
import jax.numpy as jnp
from jax import lax
from jax.experimental import pallas as pl
from jax.experimental.pallas import tpu as pltpu
from jax.sharding import PartitionSpec as P


OPS = 4
RANGE = 4
TAPS = 2 * RANGE
EVEN = tuple(a for a in range(OPS) if a % 2 == 0)
ODD = tuple(a for a in range(OPS) if a % 2 == 1)
SUB = 8
LANES = 128
VMEM = pltpu.VMEM
F32 = jnp.float32
BF16 = jnp.bfloat16
INNER_BODY = 14
MAIN_BODY = 28
VMEM_LIMIT = 24 * 1024 * 1024


def lane_index(shape):
    return lax.broadcasted_iota(jnp.int32, shape, len(shape) - 1)


def pack_kernel(parity, hop_far, right, left, bonds, near, far, side, own, value, coef, hop, vectors, bits, flat, head, tail, sems):
    count, rows, cols = right.shape
    even = parity[0] == 0
    group = LANES // TAPS
    pitch = rows + 1
    batch = 2 * SUB
    batches = count // batch

    copies = []
    for which, ref in enumerate((right, left)):
        for n in range(batches):
            copies.append((ref.at[pl.ds(n * batch, batch)], vectors.at[which, pl.ds(n * batch, batch)]))
    for a in ODD + EVEN:
        copies.append((bonds.at[a], bits.at[a]))
    copies.append((hop_far, hop))
    copies = [pltpu.make_async_copy(src, dst, sems.at[n]) for n, (src, dst) in enumerate(copies)]
    for copy in copies:
        copy.start()

    lane = lane_index((batch, cols)) // TAPS

    def pack(at, flat):
        for tile in range(rows // group):
            total = jnp.zeros((batch, cols), F32)
            for r in range(group):
                row = tile * group + r
                strip = jnp.concatenate(
                    [flat[pl.ds(half * SUB * pitch + row, SUB, stride=pitch), :] for half in range(2)], axis=0
                )
                total = jnp.where(lane == r, pltpu.roll(strip, (RANGE + TAPS * r) % LANES, 1), total)
            side[tile, at : at + batch, :] = total.astype(BF16)

    def send(at):
        for row in range(RANGE):
            def strip(ref, offset):
                parts = [ref[pl.ds((at + half * SUB) * SUB + offset, SUB, stride=SUB), :] for half in range(2)]
                return jnp.concatenate(parts, axis=0)

            low = strip(head, row)
            high = strip(tail, SUB - RANGE + row)
            near[row, at : at + batch, :] = jnp.where(even, high, low).astype(BF16)
            far[row, at : at + batch, :] = jnp.where(even, low, high).astype(BF16)

    for which in range(2):
        for n in range(batches):
            for m in range(n, n + 4 if n % 4 == 0 else n):
                copies[which * batches + m].wait()
            at = which * count + n * batch
            for v in range(batch):
                one = vectors[which, n * batch + v].astype(F32)
                start = (n * batch + v) * pitch
                value[which, start : start + rows, :] = one
                head[(at + v) * SUB : (at + v + 1) * SUB, :] = one[:SUB]
                tail[(at + v) * SUB : (at + v + 1) * SUB, :] = one[rows - SUB :]
            pack(at, value.at[which, pl.ds(n * batch * pitch, batch * pitch)])
            send(at)
    at = 2 * count
    copies[-1].wait()
    for n, a in enumerate(ODD + EVEN):
        copies[2 * batches + n].wait()
        for index in range(TAPS):
            scale = hop[a, index % RANGE] * (1.0 if index < RANGE else -1.0)
            sign = (2 * bits[a, index] - 1).astype(F32)
            coef[a * TAPS + index] = sign * scale
            if a in ODD:
                t = ODD.index(a) * TAPS + index
                flat[t * pitch : t * pitch + rows, :] = sign
            else:
                t = at + EVEN.index(a) * TAPS + index
                head[t * SUB : (t + 1) * SUB, :] = sign[:SUB]
                tail[t * SUB : (t + 1) * SUB, :] = sign[rows - SUB :]
    pack(at, flat)
    send(at)
    own[...] = side[:, at:, :]


def along_rows(which, value_at, factor_at):
    totals = {}
    for index in range(TAPS):
        step = (index % RANGE + 1) * (1 if index < RANGE else -1) * (1 if which == 0 else -1)
        moved = value_at(step)
        for a in EVEN:
            term = factor_at(a, index) * moved
            totals[a] = term if index == 0 else totals[a] + term
    return totals


def factor_row(which, row, index):
    step = index % RANGE + 1
    return row if which == 0 else row + (-step if index < RANGE else step)


def inner_kernel(value, coef, inner, along):
    _, rows, count, _ = along.shape
    cols = coef.shape[2]
    pitch = rows + 1
    period = 2 * TAPS

    tile = (period, cols)
    gap = (lane_index(tile) - lax.broadcasted_iota(jnp.int32, tile, 0)) % period
    near_diagonal = lane_index((cols, cols)) - lax.broadcasted_iota(jnp.int32, (cols, cols), 0)
    within = jnp.where((near_diagonal >= -TAPS) & (near_diagonal < TAPS), 1.0, 0.0).astype(BF16)

    def matrices(row):
        pieces = {}
        for a in ODD:
            total = jnp.zeros(tile, F32)
            for k in range(1, RANGE + 1):
                total = jnp.where(gap == period - k, coef[a * TAPS + k - 1, pl.ds(row, period, stride=0), :], total)
                total = jnp.where(gap == k, coef[a * TAPS + RANGE + k - 1, pl.ds(row, period, stride=0), :], total)
            high = total.astype(BF16)
            low = (total - high.astype(F32)).astype(BF16)
            for part, piece in enumerate((high, low)):
                pieces[part, a] = jnp.concatenate([piece] * (cols // period), axis=0) * within
        right_side = jnp.concatenate([jnp.concatenate([pieces[part, a] for a in ODD], axis=1) for part in range(2)], axis=0)
        left_side = jnp.concatenate([jnp.concatenate([pieces[part, a] for part in range(2)], axis=1) for a in ODD], axis=0)
        return right_side, left_side

    def strip(which, g, row):
        return value[which, pl.ds(g * SUB * pitch + row, SUB, stride=pitch), :]

    def columns(row):
        bands = matrices(row)
        for which in range(2):
            middle = jnp.concatenate([strip(which, g, row) for g in range(count // SUB)], axis=0).astype(BF16)
            middle = jnp.concatenate([middle, middle], axis=1)
            dims = (((1,), (which,)), ((), ()))
            along[which, row] = lax.dot_general(middle, bands[which], dims, preferred_element_type=F32)

    def lines(row):
        for which in range(2):
            factors = {}
            for a in EVEN:
                for index in range(TAPS):
                    factors[a, index] = coef[a * TAPS + index, pl.ds(factor_row(which, row, index), SUB, stride=0), :]
            for pair in range(count // (2 * SUB)):
                halves = [
                    along_rows(which, lambda step, g=2 * pair + half: strip(which, g, row + step), lambda a, index: factors[a, index])
                    for half in range(2)
                ]
                for o, a in enumerate(EVEN):
                    at = o * count + pair * 2 * SUB
                    inner[which, row, at : at + 2 * SUB, :] = jnp.concatenate([half[a] for half in halves], axis=0).astype(BF16)

    @pl.loop(0, RANGE // 2)
    def _(n):
        for one in range(2):
            columns(2 * n + one)
            columns(rows - RANGE + 2 * n + one)

    @pl.loop(0, (rows - 2 * RANGE) // INNER_BODY)
    def _(step):
        for n in range(INNER_BODY):
            row = RANGE + step * INNER_BODY + n
            columns(row)
            lines(row)


def main_kernel(widths, parity, hop, coef, value, inner, along, near, far, side, own, out, band, near_ends, ends, acc):
    _, rows, count, _ = along.shape
    cols = coef.shape[2]
    pitch = rows + 1
    even = parity[0] == 0
    group = LANES // TAPS

    def scale_of(a, index):
        return hop[a, index % RANGE] * (1.0 if index < RANGE else -1.0)

    def outer(slab, row):
        low = jnp.where(even, far[row, slab, :].astype(F32), near[row, slab, :].astype(F32))
        high = jnp.where(even, near[row, slab, :].astype(F32), far[row, slab, :].astype(F32))
        return low, high

    for row in range(RANGE):
        low, high = outer(slice(2 * count, 2 * count + 2 * SUB), row)
        for slot in range(len(EVEN) * TAPS):
            a, index = EVEN[slot // TAPS], slot % TAPS
            source = low if index < RANGE else high
            near_ends[slot, row : row + 1, :] = source[slot : slot + 1] * scale_of(a, index)

    for end in range(2):
        for n in range(RANGE):
            row = n if end == 0 else rows - RANGE + n
            for which in range(2):
                def value_at(step, base):
                    at = row + step
                    slab = slice(which * count + base, which * count + base + 2 * SUB)
                    if at < 0:
                        return outer(slab, at + RANGE)[0]
                    if at >= rows:
                        return outer(slab, at - rows)[1]
                    parts = [value[which, pl.ds((base + half * SUB) * pitch + at, SUB, stride=pitch), :] for half in range(2)]
                    return jnp.concatenate(parts, axis=0)

                def factor_at(a, index):
                    at = factor_row(which, row, index)
                    if 0 <= at < rows:
                        one = coef[a * TAPS + index, at : at + 1, :]
                    else:
                        at = at + RANGE if at < 0 else at - rows
                        one = near_ends[EVEN.index(a) * TAPS + index, at : at + 1, :]
                    return jnp.broadcast_to(one, (2 * SUB, cols))

                for base in range(0, count, 2 * SUB):
                    totals = along_rows(which, lambda step, base=base: value_at(step, base), factor_at)
                    for o, a in enumerate(EVEN):
                        at = o * count + base
                        ends[which, end * RANGE + n, at : at + 2 * SUB, :] = totals[a].astype(BF16)

    tile_shape = (count, cols)
    spot = lane_index((1, cols)) % TAPS
    spots = lane_index(tile_shape) % TAPS
    for tile in range(rows // group):
        mine = own[tile].astype(F32)
        theirs = side[tile, 2 * count :, :].astype(F32)
        for which in range(2):
            packed = side[tile, which * count : (which + 1) * count, :].astype(F32)
            total = {}
            for k in range(1, RANGE + 1):
                moved = jnp.where(spots < RANGE, pltpu.roll(packed, LANES - k, 1), pltpu.roll(packed, k, 1))
                for a in ODD:
                    slot = ODD.index(a) * TAPS + k - 1
                    if which == 0:
                        tops, bottoms = mine[slot : slot + 1], mine[slot + RANGE : slot + RANGE + 1]
                        weight = jnp.where(spot < RANGE, tops * scale_of(a, k - 1), bottoms * scale_of(a, RANGE + k - 1))
                    else:
                        tops = pltpu.roll(theirs, LANES - k, 1)[slot + RANGE : slot + RANGE + 1]
                        bottoms = pltpu.roll(theirs, k, 1)[slot : slot + 1]
                        weight = jnp.where(spot < RANGE, tops * scale_of(a, RANGE + k - 1), bottoms * scale_of(a, k - 1))
                    valid = ((spot < RANGE) & (spot + k >= RANGE)) | ((spot >= RANGE) & (spot - k < RANGE))
                    term = jnp.where(valid, weight, 0.0) * moved
                    total[a] = term if k == 1 else total[a] + term
            for a in ODD:
                band[which, ODD.index(a), tile] = total[a]

    acc[...] = jnp.zeros_like(acc)
    rim_lane = (lane_index(tile_shape) < RANGE) | (lane_index(tile_shape) >= cols - RANGE)

    def results(row, even_of):
        found = []
        tile = row // group
        turn = (2 * LANES - RANGE - TAPS * (row % group)) % LANES
        for which in range(2):
            both = along[which, row]
            done = {a: even_of(which)[EVEN.index(a) * count : (EVEN.index(a) + 1) * count] for a in EVEN}
            for o, a in enumerate(ODD):
                beyond = jnp.where(rim_lane, pltpu.roll(band[which, o, tile], turn, 1), 0.0)
                done[a] = (both[:, o * cols : (o + 1) * cols] + beyond).astype(BF16)
            found.append(jnp.concatenate([done[a] for a in range(OPS)], axis=0))
        return found

    def accumulate(pairs):
        for pair in pairs:
            found = [results(*one) for one in pair]
            first = jnp.concatenate([one[0] for one in found], axis=1)
            back = jnp.concatenate([one[1] for one in found], axis=1)
            acc[...] += lax.dot_general(back, first, (((1,), (1,)), ((), ())), preferred_element_type=F32)

    def end_row(n):
        return (n if n < RANGE else rows - 2 * RANGE + n), lambda which: ends[which, n]

    accumulate([[end_row(n), end_row(n + 1)] for n in range(0, 2 * RANGE, 2)])

    @pl.loop(0, (rows - 2 * RANGE) // MAIN_BODY)
    def _(step):
        def inner_row(n):
            row = RANGE + step * MAIN_BODY + n
            return row, lambda which: inner[which, row]

        accumulate([[inner_row(n), inner_row(n + 1)] for n in range(0, MAIN_BODY, 2)])

    parts_left, parts_right = widths
    per_left, per_right = count // parts_left, count // parts_right
    size = OPS * count

    def order(per, dim):
        new = lax.broadcasted_iota(jnp.int32, (size, size), dim)
        old = lax.broadcasted_iota(jnp.int32, (size, size), 1 - dim)
        part, rest = new // (OPS * per), new % (OPS * per)
        return jnp.where(old == (rest // per) * count + part * per + rest % per, 1.0, 0.0).astype(BF16)

    moved = jnp.dot(order(per_left, 0), acc[...].astype(BF16), preferred_element_type=F32).astype(BF16)
    moved = jnp.dot(moved, order(per_right, 1), preferred_element_type=F32).astype(BF16)
    if out.ndim == 2:
        out[...] = moved
    else:
        width = OPS * per_right
        for d in range(parts_left * parts_right):
            w, r = divmod(d, parts_right)
            out[d] = moved[w * OPS * per_left : (w + 1) * OPS * per_left, r * width : (r + 1) * width]


def sum_kernel(factor, got, out):
    total = jnp.sum(got[...].astype(F32), axis=0) * factor
    per_left, per_right = out.shape[1], out.shape[2]
    for a in range(OPS):
        for b in range(OPS):
            out[a * OPS + b] = total[a * per_left : (a + 1) * per_left, b * per_right : (b + 1) * per_right]


def swap(array, axis, pairs):
    return lax.ppermute(array, axis, pairs)


def on_device(left, right, bond_signs, hop):
    count, rows, cols = right.shape
    wide, narrow = lax.axis_size("wide"), lax.axis_size("narrow")
    edge_rows = 2 * count + len(EVEN) * TAPS
    side_rows = 2 * count + len(ODD) * TAPS
    tiles = rows * TAPS // LANES
    parity = (lax.axis_index("wide") % 2).astype(jnp.int32).reshape(1)
    smem = pl.BlockSpec(memory_space=pltpu.SMEM)
    vmem = pl.BlockSpec(memory_space=pltpu.VMEM)
    params = pltpu.CompilerParams(vmem_limit_bytes=VMEM_LIMIT)

    hbm = pl.BlockSpec(memory_space=pltpu.HBM)

    near, far, side, own, value, coef = pl.pallas_call(
        pack_kernel,
        out_shape=(
            jax.ShapeDtypeStruct((RANGE, edge_rows, cols), BF16),
            jax.ShapeDtypeStruct((RANGE, edge_rows, cols), BF16),
            jax.ShapeDtypeStruct((tiles, side_rows, cols), BF16),
            jax.ShapeDtypeStruct((tiles, side_rows - 2 * count, cols), BF16),
            jax.ShapeDtypeStruct((2, count * (rows + 1), cols), F32),
            jax.ShapeDtypeStruct((OPS * TAPS, rows, cols), F32),
        ),
        in_specs=[smem, hbm, hbm, hbm, hbm],
        out_specs=(vmem,) * 6,
        scratch_shapes=[
            pltpu.SMEM((OPS, RANGE), F32),
            VMEM((2, count, rows, cols), BF16),
            VMEM((OPS, TAPS, rows, cols), jnp.int32),
            VMEM((2 * SUB * (rows + 1), cols), F32),
            VMEM((edge_rows * SUB, cols), F32),
            VMEM((edge_rows * SUB, cols), F32),
            pltpu.SemaphoreType.DMA((2 * (count // (2 * SUB)) + OPS + 1,)),
        ],
        compiler_params=params,
        name="pack",
    )(parity, *(pltpu.with_memory_space_constraint(one, pltpu.HBM) for one in (hop, right, left, bond_signs)))
    inner, along = pl.pallas_call(
        inner_kernel,
        out_shape=(
            jax.ShapeDtypeStruct((2, rows, len(EVEN) * count, cols), BF16),
            jax.ShapeDtypeStruct((2, rows, count, len(ODD) * cols), F32),
        ),
        in_specs=[vmem, vmem],
        out_specs=(vmem,) * 2,
        compiler_params=params,
        name="interior",
    )(value, coef)

    far = swap(far, "wide", [(i, (i + 1) % wide if i % 2 else (i - 1) % wide) for i in range(wide)])
    near = swap(near, "wide", [(i, i ^ 1) for i in range(wide)])
    if narrow == 2:
        side = swap(side, "narrow", [(0, 1), (1, 0)])
    else:
        before = swap(side, "narrow", [(i, (i + 1) % narrow) for i in range(narrow)])
        after = swap(side, "narrow", [((i + 1) % narrow, i) for i in range(narrow)])
        side = jnp.where(lane_index(side.shape) % TAPS < RANGE, before, after)

    per_left, per_right = count // wide, count // narrow
    size = OPS * count
    direct = (OPS * per_right) % LANES == 0 and (OPS * per_left) % 16 == 0
    blocked = (wide * narrow, OPS * per_left, OPS * per_right)
    partial = pl.pallas_call(
        lambda *refs: main_kernel((wide, narrow), *refs),
        out_shape=jax.ShapeDtypeStruct(blocked if direct else (size, size), BF16),
        in_specs=[smem, smem] + [vmem] * 8,
        out_specs=vmem,
        scratch_shapes=[
            VMEM((2, len(ODD), tiles, count, cols), F32),
            VMEM((len(EVEN) * TAPS, RANGE, cols), F32),
            VMEM((2, 2 * RANGE, len(EVEN) * count, cols), BF16),
            VMEM((size, size), F32),
        ],
        compiler_params=params,
        name="moments",
    )(parity, hop, coef, value, inner, along, near, far, side, own)
    if not direct:
        partial = partial.reshape(wide, OPS * per_left, narrow, OPS * per_right).transpose(0, 2, 1, 3).reshape(blocked)
    got = lax.all_to_all(partial, ("wide", "narrow"), 0, 0, tiled=True)
    factor = 1.0 / math.sqrt(rows * cols * wide * narrow)
    return pl.pallas_call(
        lambda *refs: sum_kernel(factor, *refs),
        out_shape=jax.ShapeDtypeStruct((OPS * OPS, per_left, per_right), F32),
        in_specs=[vmem],
        out_specs=vmem,
        compiler_params=params,
        name="total",
    )(got)


def solution(mesh):
    in_specs = (
        P(None, "wide", "narrow"),
        P(None, "wide", "narrow"),
        P(None, None, "wide", "narrow"),
        P(),
    )
    out_specs = P(None, "wide", "narrow")

    return jax.shard_map(on_device, mesh=mesh, in_specs=in_specs, out_specs=out_specs, check_vma=False)
```

```python
import math

import jax
import jax.numpy as jnp
from jax import lax
from jax.experimental import pallas as pl
from jax.experimental.pallas import tpu as pltpu
from jax.sharding import PartitionSpec as P


OPS = 4
RANGE = 4
TAPS = 2 * RANGE
EVEN = tuple(a for a in range(OPS) if a % 2 == 0)
ODD = tuple(a for a in range(OPS) if a % 2 == 1)
SUB = 8
LANES = 128
VMEM = pltpu.VMEM
F32 = jnp.float32
BF16 = jnp.bfloat16
INNER_BODY = 28
INNER_LEAD = 6
MAIN_BODY = 28
VMEM_LIMIT = 24 * 1024 * 1024


def lane_index(shape):
    return lax.broadcasted_iota(jnp.int32, shape, len(shape) - 1)


def pack_kernel(parity, hop_far, right, left, bonds, near, far, side, own, value, coef, hop, vectors, bits, flat, head, tail, sems):
    count, rows, cols = right.shape
    even = parity[0] == 0
    group = LANES // TAPS
    pitch = rows + 1
    batch = 2 * SUB
    batches = count // batch

    copies = []
    for which, ref in enumerate((right, left)):
        for n in range(batches):
            copies.append((ref.at[pl.ds(n * batch, batch)], vectors.at[which, pl.ds(n * batch, batch)]))
    for a in ODD + EVEN:
        copies.append((bonds.at[a], bits.at[a]))
    copies.append((hop_far, hop))
    copies = [pltpu.make_async_copy(src, dst, sems.at[n]) for n, (src, dst) in enumerate(copies)]
    for copy in copies:
        copy.start()

    lane = lane_index((batch, cols)) // TAPS

    def pack(at, flat):
        for tile in range(rows // group):
            total = jnp.zeros((batch, cols), F32)
            for r in range(group):
                row = tile * group + r
                strip = jnp.concatenate(
                    [flat[pl.ds(half * SUB * pitch + row, SUB, stride=pitch), :] for half in range(2)], axis=0
                )
                total = jnp.where(lane == r, pltpu.roll(strip, (RANGE + TAPS * r) % LANES, 1), total)
            side[tile, at : at + batch, :] = total.astype(BF16)

    def send(at):
        for row in range(RANGE):
            def strip(ref, offset):
                parts = [ref[pl.ds((at + half * SUB) * SUB + offset, SUB, stride=SUB), :] for half in range(2)]
                return jnp.concatenate(parts, axis=0)

            low = strip(head, row)
            high = strip(tail, SUB - RANGE + row)
            near[row, at : at + batch, :] = jnp.where(even, high, low).astype(BF16)
            far[row, at : at + batch, :] = jnp.where(even, low, high).astype(BF16)

    for which in range(2):
        for n in range(batches):
            for m in range(n, n + 4 if n % 4 == 0 else n):
                copies[which * batches + m].wait()
            at = which * count + n * batch
            for v in range(batch):
                one = vectors[which, n * batch + v].astype(F32)
                start = (n * batch + v) * pitch
                value[which, start : start + rows, :] = one
                head[(at + v) * SUB : (at + v + 1) * SUB, :] = one[:SUB]
                tail[(at + v) * SUB : (at + v + 1) * SUB, :] = one[rows - SUB :]
            pack(at, value.at[which, pl.ds(n * batch * pitch, (batch + SUB) * pitch)])
            send(at)
    at = 2 * count
    copies[-1].wait()
    for n, a in enumerate(ODD + EVEN):
        copies[2 * batches + n].wait()
        for index in range(TAPS):
            scale = hop[a, index % RANGE] * (1.0 if index < RANGE else -1.0)
            sign = (2 * bits[a, index] - 1).astype(F32)
            coef[a * TAPS + index, :rows, :] = sign * scale
            if a in ODD:
                t = ODD.index(a) * TAPS + index
                flat[t * pitch : t * pitch + rows, :] = sign
            else:
                t = at + EVEN.index(a) * TAPS + index
                head[t * SUB : (t + 1) * SUB, :] = sign[:SUB]
                tail[t * SUB : (t + 1) * SUB, :] = sign[rows - SUB :]
    pack(at, flat)
    send(at)
    own[...] = side[:, at:, :]


def along_rows(which, value_at, factor_at):
    totals = {}
    for index in range(TAPS):
        step = (index % RANGE + 1) * (1 if index < RANGE else -1) * (1 if which == 0 else -1)
        moved = value_at(step)
        for a in EVEN:
            term = factor_at(a, index) * moved
            totals[a] = term if index == 0 else totals[a] + term
    return totals


def factor_row(which, row, index):
    step = index % RANGE + 1
    return row if which == 0 else row + (-step if index < RANGE else step)


def inner_kernel(value, coef, inner, along):
    _, rows, count, _ = along.shape
    cols = coef.shape[2]
    pitch = rows + 1
    period = 2 * TAPS

    tile = (period, cols)
    gap = (lane_index(tile) - lax.broadcasted_iota(jnp.int32, tile, 0)) % period
    near_diagonal = lane_index((cols, cols)) - lax.broadcasted_iota(jnp.int32, (cols, cols), 0)
    within = jnp.where((near_diagonal >= -TAPS) & (near_diagonal < TAPS), 1.0, 0.0).astype(BF16)

    def matrices(row):
        pieces = {}
        for a in ODD:
            total = jnp.zeros(tile, F32)
            for k in range(1, RANGE + 1):
                total = jnp.where(gap == period - k, coef[a * TAPS + k - 1, pl.ds(row, period, stride=0), :], total)
                total = jnp.where(gap == k, coef[a * TAPS + RANGE + k - 1, pl.ds(row, period, stride=0), :], total)
            high = total.astype(BF16)
            low = (total - high.astype(F32)).astype(BF16)
            for part, piece in enumerate((high, low)):
                pieces[part, a] = jnp.concatenate([piece] * (cols // period), axis=0) * within
        right_side = jnp.concatenate([jnp.concatenate([pieces[part, a] for a in ODD], axis=1) for part in range(2)], axis=0)
        left_side = jnp.concatenate([jnp.concatenate([pieces[part, a] for part in range(2)], axis=1) for a in ODD], axis=0)
        return right_side, left_side

    def strip(which, g, row):
        return value[which, pl.ds(g * SUB * pitch + row, SUB, stride=pitch), :]

    def columns(row):
        bands = matrices(row)
        for which in range(2):
            middle = jnp.concatenate([strip(which, g, row) for g in range(count // SUB)], axis=0).astype(BF16)
            middle = jnp.concatenate([middle, middle], axis=1)
            dims = (((1,), (which,)), ((), ()))
            along[which, row] = lax.dot_general(middle, bands[which], dims, preferred_element_type=F32)

    def lines(row):
        for which in range(2):
            factors = {}
            for a in EVEN:
                for index in range(TAPS):
                    factors[a, index] = coef[a * TAPS + index, pl.ds(factor_row(which, row, index), SUB, stride=0), :]
            for pair in range(count // (2 * SUB)):
                halves = [
                    along_rows(which, lambda step, g=2 * pair + half: strip(which, g, row + step), lambda a, index: factors[a, index])
                    for half in range(2)
                ]
                for o, a in enumerate(EVEN):
                    at = o * count + pair * 2 * SUB
                    inner[which, row, at : at + 2 * SUB, :] = jnp.concatenate([half[a] for half in halves], axis=0).astype(BF16)

    trips = (rows - 2 * RANGE) // INNER_BODY
    each = rows // trips

    @pl.loop(0, trips)
    def _(step):
        for n in range(each):
            columns(step * each + n)
            if n >= INNER_LEAD:
                lines(RANGE + step * INNER_BODY + n - INNER_LEAD)
        for n in range(each - INNER_LEAD, INNER_BODY):
            lines(RANGE + step * INNER_BODY + n)


def main_kernel(widths, parity, hop, coef, value, inner, along, near, far, side, own, out, band, near_ends, ends, acc):
    _, rows, count, _ = along.shape
    cols = coef.shape[2]
    pitch = rows + 1
    even = parity[0] == 0
    group = LANES // TAPS

    def scale_of(a, index):
        return hop[a, index % RANGE] * (1.0 if index < RANGE else -1.0)

    def outer(slab, row):
        low = jnp.where(even, far[row, slab, :].astype(F32), near[row, slab, :].astype(F32))
        high = jnp.where(even, near[row, slab, :].astype(F32), far[row, slab, :].astype(F32))
        return low, high

    for row in range(RANGE):
        low, high = outer(slice(2 * count, 2 * count + 2 * SUB), row)
        for slot in range(len(EVEN) * TAPS):
            a, index = EVEN[slot // TAPS], slot % TAPS
            source = low if index < RANGE else high
            near_ends[slot, row : row + 1, :] = source[slot : slot + 1] * scale_of(a, index)

    for end in range(2):
        for n in range(RANGE):
            row = n if end == 0 else rows - RANGE + n
            for which in range(2):
                def value_at(step, base):
                    at = row + step
                    slab = slice(which * count + base, which * count + base + 2 * SUB)
                    if at < 0:
                        return outer(slab, at + RANGE)[0]
                    if at >= rows:
                        return outer(slab, at - rows)[1]
                    parts = [value[which, pl.ds((base + half * SUB) * pitch + at, SUB, stride=pitch), :] for half in range(2)]
                    return jnp.concatenate(parts, axis=0)

                def factor_at(a, index):
                    at = factor_row(which, row, index)
                    if 0 <= at < rows:
                        one = coef[a * TAPS + index, at : at + 1, :]
                    else:
                        at = at + RANGE if at < 0 else at - rows
                        one = near_ends[EVEN.index(a) * TAPS + index, at : at + 1, :]
                    return jnp.broadcast_to(one, (2 * SUB, cols))

                for base in range(0, count, 2 * SUB):
                    totals = along_rows(which, lambda step, base=base: value_at(step, base), factor_at)
                    for o, a in enumerate(EVEN):
                        at = o * count + base
                        ends[which, end * RANGE + n, at : at + 2 * SUB, :] = totals[a].astype(BF16)

    tile_shape = (count, cols)
    spot = lane_index((1, cols)) % TAPS
    spots = lane_index(tile_shape) % TAPS
    for tile in range(rows // group):
        mine = own[tile].astype(F32)
        theirs = side[tile, 2 * count :, :].astype(F32)
        for which in range(2):
            packed = side[tile, which * count : (which + 1) * count, :]
            total = {}
            for k in range(1, RANGE + 1):
                moved = jnp.where(spots < RANGE, pltpu.roll(packed, LANES - k, 1).astype(F32), pltpu.roll(packed, k, 1).astype(F32))
                for a in ODD:
                    slot = ODD.index(a) * TAPS + k - 1
                    if which == 0:
                        tops, bottoms = mine[slot : slot + 1], mine[slot + RANGE : slot + RANGE + 1]
                        weight = jnp.where(spot < RANGE, tops * scale_of(a, k - 1), bottoms * scale_of(a, RANGE + k - 1))
                    else:
                        tops = pltpu.roll(theirs, LANES - k, 1)[slot + RANGE : slot + RANGE + 1]
                        bottoms = pltpu.roll(theirs, k, 1)[slot : slot + 1]
                        weight = jnp.where(spot < RANGE, tops * scale_of(a, RANGE + k - 1), bottoms * scale_of(a, k - 1))
                    valid = ((spot < RANGE) & (spot + k >= RANGE)) | ((spot >= RANGE) & (spot - k < RANGE))
                    term = jnp.where(valid, weight, 0.0) * moved
                    total[a] = term if k == 1 else total[a] + term
            for a in ODD:
                band[which, ODD.index(a), tile] = total[a].astype(BF16)

    acc[...] = jnp.zeros_like(acc)
    rim_lane = (lane_index(tile_shape) < RANGE) | (lane_index(tile_shape) >= cols - RANGE)

    def results(row, even_of):
        found = []
        tile = row // group
        turn = (2 * LANES - RANGE - TAPS * (row % group)) % LANES
        for which in range(2):
            both = along[which, row]
            done = {a: even_of(which)[EVEN.index(a) * count : (EVEN.index(a) + 1) * count] for a in EVEN}
            for o, a in enumerate(ODD):
                beyond = jnp.where(rim_lane, pltpu.roll(band[which, o, tile], turn, 1).astype(F32), 0.0)
                done[a] = (both[:, o * cols : (o + 1) * cols] + beyond).astype(BF16)
            found.append(jnp.concatenate([done[a] for a in range(OPS)], axis=0))
        return found

    def accumulate(pairs):
        for pair in pairs:
            found = [results(*one) for one in pair]
            first = jnp.concatenate([one[0] for one in found], axis=1)
            back = jnp.concatenate([one[1] for one in found], axis=1)
            acc[...] += lax.dot_general(back, first, (((1,), (1,)), ((), ())), preferred_element_type=F32)

    def end_row(n):
        return (n if n < RANGE else rows - 2 * RANGE + n), lambda which: ends[which, n]

    accumulate([[end_row(n), end_row(n + 1)] for n in range(0, 2 * RANGE, 2)])

    @pl.loop(0, (rows - 2 * RANGE) // MAIN_BODY)
    def _(step):
        def inner_row(n):
            row = RANGE + step * MAIN_BODY + n
            return row, lambda which: inner[which, row]

        accumulate([[inner_row(n), inner_row(n + 1)] for n in range(0, MAIN_BODY, 2)])

    parts_left, parts_right = widths
    per_left, per_right = count // parts_left, count // parts_right
    size = OPS * count

    def order(per, dim):
        new = lax.broadcasted_iota(jnp.int32, (size, size), dim)
        old = lax.broadcasted_iota(jnp.int32, (size, size), 1 - dim)
        part, rest = new // (OPS * per), new % (OPS * per)
        return jnp.where(old == (rest // per) * count + part * per + rest % per, 1.0, 0.0).astype(BF16)

    moved = jnp.dot(order(per_left, 0), acc[...].astype(BF16), preferred_element_type=F32).astype(BF16)
    moved = jnp.dot(moved, order(per_right, 1), preferred_element_type=F32).astype(BF16)
    if out.ndim == 2:
        out[...] = moved
    else:
        width = OPS * per_right
        for d in range(parts_left * parts_right):
            w, r = divmod(d, parts_right)
            out[d] = moved[w * OPS * per_left : (w + 1) * OPS * per_left, r * width : (r + 1) * width]


def sum_kernel(factor, got, out):
    total = jnp.sum(got[...].astype(F32), axis=0) * factor
    per_left, per_right = out.shape[1], out.shape[2]
    for a in range(OPS):
        for b in range(OPS):
            out[a * OPS + b] = total[a * per_left : (a + 1) * per_left, b * per_right : (b + 1) * per_right]


def swap(array, axis, pairs):
    return lax.ppermute(array, axis, pairs)


def on_device(left, right, bond_signs, hop):
    count, rows, cols = right.shape
    wide, narrow = lax.axis_size("wide"), lax.axis_size("narrow")
    edge_rows = 2 * count + len(EVEN) * TAPS
    side_rows = 2 * count + len(ODD) * TAPS
    tiles = rows * TAPS // LANES
    parity = (lax.axis_index("wide") % 2).astype(jnp.int32).reshape(1)
    smem = pl.BlockSpec(memory_space=pltpu.SMEM)
    vmem = pl.BlockSpec(memory_space=pltpu.VMEM)
    params = pltpu.CompilerParams(vmem_limit_bytes=VMEM_LIMIT)

    hbm = pl.BlockSpec(memory_space=pltpu.HBM)

    near, far, side, own, value, coef = pl.pallas_call(
        pack_kernel,
        out_shape=(
            jax.ShapeDtypeStruct((RANGE, edge_rows, cols), BF16),
            jax.ShapeDtypeStruct((RANGE, edge_rows, cols), BF16),
            jax.ShapeDtypeStruct((tiles, side_rows, cols), BF16),
            jax.ShapeDtypeStruct((tiles, side_rows - 2 * count, cols), BF16),
            jax.ShapeDtypeStruct((2, (count + SUB) * (rows + 1), cols), F32),
            jax.ShapeDtypeStruct((OPS * TAPS, rows + 2 * SUB, cols), F32),
        ),
        in_specs=[smem, hbm, hbm, hbm, hbm],
        out_specs=(vmem,) * 6,
        scratch_shapes=[
            pltpu.SMEM((OPS, RANGE), F32),
            VMEM((2, count, rows, cols), BF16),
            VMEM((OPS, TAPS, rows, cols), jnp.int32),
            VMEM((3 * SUB * (rows + 1), cols), F32),
            VMEM((edge_rows * SUB + SUB, cols), F32),
            VMEM((edge_rows * SUB + SUB, cols), F32),
            pltpu.SemaphoreType.DMA((2 * (count // (2 * SUB)) + OPS + 1,)),
        ],
        compiler_params=params,
        name="pack",
    )(parity, *(pltpu.with_memory_space_constraint(one, pltpu.HBM) for one in (hop, right, left, bond_signs)))
    inner, along = pl.pallas_call(
        inner_kernel,
        out_shape=(
            jax.ShapeDtypeStruct((2, rows, len(EVEN) * count, cols), BF16),
            jax.ShapeDtypeStruct((2, rows, count, len(ODD) * cols), F32),
        ),
        in_specs=[vmem, vmem],
        out_specs=(vmem,) * 2,
        compiler_params=params,
        name="interior",
    )(value, coef)

    far = swap(far, "wide", [(i, (i + 1) % wide if i % 2 else (i - 1) % wide) for i in range(wide)])
    near = swap(near, "wide", [(i, i ^ 1) for i in range(wide)])
    if narrow == 2:
        side = swap(side, "narrow", [(0, 1), (1, 0)])
    else:
        before = swap(side, "narrow", [(i, (i + 1) % narrow) for i in range(narrow)])
        after = swap(side, "narrow", [((i + 1) % narrow, i) for i in range(narrow)])
        side = jnp.where(lane_index(side.shape) % TAPS < RANGE, before, after)

    per_left, per_right = count // wide, count // narrow
    size = OPS * count
    direct = (OPS * per_right) % LANES == 0 and (OPS * per_left) % 16 == 0
    blocked = (wide * narrow, OPS * per_left, OPS * per_right)
    partial = pl.pallas_call(
        lambda *refs: main_kernel((wide, narrow), *refs),
        out_shape=jax.ShapeDtypeStruct(blocked if direct else (size, size), BF16),
        in_specs=[smem, smem] + [vmem] * 8,
        out_specs=vmem,
        scratch_shapes=[
            VMEM((2, len(ODD), tiles, count, cols), BF16),
            VMEM((len(EVEN) * TAPS, RANGE, cols), F32),
            VMEM((2, 2 * RANGE, len(EVEN) * count, cols), BF16),
            VMEM((size, size), F32),
        ],
        compiler_params=params,
        name="moments",
    )(parity, hop, coef, value, inner, along, near, far, side, own)
    if not direct:
        partial = partial.reshape(wide, OPS * per_left, narrow, OPS * per_right).transpose(0, 2, 1, 3).reshape(blocked)
    got = lax.all_to_all(partial, ("wide", "narrow"), 0, 0, tiled=True)
    factor = 1.0 / math.sqrt(rows * cols * wide * narrow)
    return pl.pallas_call(
        lambda *refs: sum_kernel(factor, *refs),
        out_shape=jax.ShapeDtypeStruct((OPS * OPS, per_left, per_right), F32),
        in_specs=[vmem],
        out_specs=vmem,
        compiler_params=params,
        name="total",
    )(got)


def solution(mesh):
    in_specs = (
        P(None, "wide", "narrow"),
        P(None, "wide", "narrow"),
        P(None, None, "wide", "narrow"),
        P(),
    )
    out_specs = P(None, "wide", "narrow")

    return jax.shard_map(on_device, mesh=mesh, in_specs=in_specs, out_specs=out_specs, check_vma=False)
```

```python
import math

import jax
import jax.numpy as jnp
from jax import lax
from jax.experimental import pallas as pl
from jax.experimental.pallas import tpu as pltpu
from jax.sharding import PartitionSpec as P


OPS = 4
RANGE = 4
TAPS = 2 * RANGE
EVEN = tuple(a for a in range(OPS) if a % 2 == 0)
ODD = tuple(a for a in range(OPS) if a % 2 == 1)
SUB = 8
LANES = 128
VMEM = pltpu.VMEM
F32 = jnp.float32
BF16 = jnp.bfloat16
INNER_BODY = 28
INNER_LEAD = 6
VMEM_LIMIT = 24 * 1024 * 1024


def lane_index(shape):
    return lax.broadcasted_iota(jnp.int32, shape, len(shape) - 1)


def pack_kernel(widths, parity, hop_far, right, left, bonds, near, far, side, own, value, coef, orders, hop, vectors, bits, flat, head, tail, sems):
    count, rows, cols = right.shape
    even = parity[0] == 0
    group = LANES // TAPS
    pitch = rows + 1
    batch = 2 * SUB
    batches = count // batch

    copies = []
    for which, ref in enumerate((right, left)):
        for n in range(batches):
            copies.append((ref.at[pl.ds(n * batch, batch)], vectors.at[which, pl.ds(n * batch, batch)]))
    for a in ODD + EVEN:
        copies.append((bonds.at[a], bits.at[a]))
    copies.append((hop_far, hop))
    copies = [pltpu.make_async_copy(src, dst, sems.at[n]) for n, (src, dst) in enumerate(copies)]
    for copy in copies:
        copy.start()

    size = OPS * count

    def order(parts, dim):
        per = count // parts
        new = lax.broadcasted_iota(jnp.int32, (size, size), dim)
        old = lax.broadcasted_iota(jnp.int32, (size, size), 1 - dim)
        part, rest = new // (OPS * per), new % (OPS * per)
        return jnp.where(old == (rest // per) * count + part * per + rest % per, 1.0, 0.0).astype(BF16)

    for dim in range(2):
        orders[dim] = order(widths[dim], dim)

    lane = lane_index((batch, cols)) // TAPS

    def pack(at, flat):
        for tile in range(rows // group):
            total = jnp.zeros((batch, cols), F32)
            for r in range(group):
                row = tile * group + r
                strip = jnp.concatenate(
                    [flat[pl.ds(half * SUB * pitch + row, SUB, stride=pitch), :] for half in range(2)], axis=0
                )
                total = jnp.where(lane == r, pltpu.roll(strip, (RANGE + TAPS * r) % LANES, 1), total)
            side[tile, at : at + batch, :] = total.astype(BF16)

    def send(at):
        for row in range(RANGE):
            def strip(ref, offset):
                parts = [ref[pl.ds((at + half * SUB) * SUB + offset, SUB, stride=SUB), :] for half in range(2)]
                return jnp.concatenate(parts, axis=0)

            low = strip(head, row)
            high = strip(tail, SUB - RANGE + row)
            near[row, at : at + batch, :] = jnp.where(even, high, low).astype(BF16)
            far[row, at : at + batch, :] = jnp.where(even, low, high).astype(BF16)

    for which in range(2):
        for n in range(batches):
            for m in range(n, n + 4 if n % 4 == 0 else n):
                copies[which * batches + m].wait()
            at = which * count + n * batch
            for v in range(batch):
                one = vectors[which, n * batch + v].astype(F32)
                start = (n * batch + v) * pitch
                value[which, start : start + rows, :] = one
                head[(at + v) * SUB : (at + v + 1) * SUB, :] = one[:SUB]
                tail[(at + v) * SUB : (at + v + 1) * SUB, :] = one[rows - SUB :]
            pack(at, value.at[which, pl.ds(n * batch * pitch, (batch + SUB) * pitch)])
            send(at)
    at = 2 * count
    copies[-1].wait()
    for n, a in enumerate(ODD + EVEN):
        copies[2 * batches + n].wait()
        for index in range(TAPS):
            scale = hop[a, index % RANGE] * (1.0 if index < RANGE else -1.0)
            sign = (2 * bits[a, index] - 1).astype(F32)
            coef[a * TAPS + index, :rows, :] = sign * scale
            if a in ODD:
                t = ODD.index(a) * TAPS + index
                flat[t * pitch : t * pitch + rows, :] = sign
            else:
                t = at + EVEN.index(a) * TAPS + index
                head[t * SUB : (t + 1) * SUB, :] = sign[:SUB]
                tail[t * SUB : (t + 1) * SUB, :] = sign[rows - SUB :]
    pack(at, flat)
    send(at)
    own[...] = side[:, at:, :]


def along_rows(which, value_at, factor_at):
    totals = {}
    for index in range(TAPS):
        step = (index % RANGE + 1) * (1 if index < RANGE else -1) * (1 if which == 0 else -1)
        moved = value_at(step)
        for a in EVEN:
            term = factor_at(a, index) * moved
            totals[a] = term if index == 0 else totals[a] + term
    return totals


def factor_row(which, row, index):
    step = index % RANGE + 1
    return row if which == 0 else row + (-step if index < RANGE else step)


def inner_kernel(value, coef, inner, along):
    _, rows, count, _ = along.shape
    cols = coef.shape[2]
    pitch = rows + 1
    period = 2 * TAPS

    tile = (period, cols)
    gap = (lane_index(tile) - lax.broadcasted_iota(jnp.int32, tile, 0)) % period
    near_diagonal = lane_index((cols, cols)) - lax.broadcasted_iota(jnp.int32, (cols, cols), 0)
    within = jnp.where((near_diagonal >= -TAPS) & (near_diagonal < TAPS), 1.0, 0.0).astype(BF16)

    def matrices(row):
        pieces = {}
        for a in ODD:
            total = jnp.zeros(tile, F32)
            for k in range(1, RANGE + 1):
                total = jnp.where(gap == period - k, coef[a * TAPS + k - 1, pl.ds(row, period, stride=0), :], total)
                total = jnp.where(gap == k, coef[a * TAPS + RANGE + k - 1, pl.ds(row, period, stride=0), :], total)
            high = total.astype(BF16)
            low = (total - high.astype(F32)).astype(BF16)
            for part, piece in enumerate((high, low)):
                pieces[part, a] = jnp.concatenate([piece] * (cols // period), axis=0) * within
        right_side = jnp.concatenate([jnp.concatenate([pieces[part, a] for a in ODD], axis=1) for part in range(2)], axis=0)
        left_side = jnp.concatenate([jnp.concatenate([pieces[part, a] for part in range(2)], axis=1) for a in ODD], axis=0)
        return right_side, left_side

    def strip(which, g, row):
        return value[which, pl.ds(g * SUB * pitch + row, SUB, stride=pitch), :]

    def columns(row):
        bands = matrices(row)
        for which in range(2):
            middle = jnp.concatenate([strip(which, g, row) for g in range(count // SUB)], axis=0).astype(BF16)
            middle = jnp.concatenate([middle, middle], axis=1)
            dims = (((1,), (which,)), ((), ()))
            along[which, row] = lax.dot_general(middle, bands[which], dims, preferred_element_type=F32)

    def lines(row):
        for which in range(2):
            factors = {}
            for a in EVEN:
                for index in range(TAPS):
                    factors[a, index] = coef[a * TAPS + index, pl.ds(factor_row(which, row, index), SUB, stride=0), :]
            for pair in range(count // (2 * SUB)):
                halves = [
                    along_rows(which, lambda step, g=2 * pair + half: strip(which, g, row + step), lambda a, index: factors[a, index])
                    for half in range(2)
                ]
                for o, a in enumerate(EVEN):
                    at = o * count + pair * 2 * SUB
                    inner[which, row, at : at + 2 * SUB, :] = jnp.concatenate([half[a] for half in halves], axis=0).astype(BF16)

    trips = (rows - 2 * RANGE) // INNER_BODY
    each = rows // trips

    @pl.loop(0, trips)
    def _(step):
        for n in range(each):
            columns(step * each + n)
            if n >= INNER_LEAD:
                lines(RANGE + step * INNER_BODY + n - INNER_LEAD)
        for n in range(each - INNER_LEAD, INNER_BODY):
            lines(RANGE + step * INNER_BODY + n)


def main_kernel(widths, parity, hop, coef, value, inner, along, near, far, side, own, orders, out, band, beyond_rows, near_ends, ends, acc):
    _, rows, count, _ = along.shape
    cols = coef.shape[2]
    pitch = rows + 1
    even = parity[0] == 0
    group = LANES // TAPS

    def scale_of(a, index):
        return hop[a, index % RANGE] * (1.0 if index < RANGE else -1.0)

    beyond_rows[0] = jnp.where(even, far[...], near[...])
    beyond_rows[1] = jnp.where(even, near[...], far[...])

    def outer(slab, row):
        return [beyond_rows[end, row, slab, :].astype(F32) for end in range(2)]

    for row in range(RANGE):
        low, high = outer(slice(2 * count, 2 * count + 2 * SUB), row)
        for slot in range(len(EVEN) * TAPS):
            a, index = EVEN[slot // TAPS], slot % TAPS
            source = low if index < RANGE else high
            near_ends[slot, row : row + 1, :] = source[slot : slot + 1] * scale_of(a, index)

    def end_piece(end, n, which, base):
        row = n if end == 0 else rows - RANGE + n
        slab = slice(which * count + base, which * count + base + 2 * SUB)

        def value_at(step):
            at = row + step
            if at < 0:
                return outer(slab, at + RANGE)[0]
            if at >= rows:
                return outer(slab, at - rows)[1]
            parts = [value[which, pl.ds((base + half * SUB) * pitch + at, SUB, stride=pitch), :] for half in range(2)]
            return jnp.concatenate(parts, axis=0)

        def factor_at(a, index):
            at = factor_row(which, row, index)
            if 0 <= at < rows:
                return coef[a * TAPS + index, pl.ds(at, 2 * SUB, stride=0), :]
            at = at + RANGE if at < 0 else at - rows
            return near_ends[EVEN.index(a) * TAPS + index, pl.ds(at, 2 * SUB, stride=0), :]

        totals = along_rows(which, value_at, factor_at)
        for o, a in enumerate(EVEN):
            at = o * count + base
            ends[which, end * RANGE + n, at : at + 2 * SUB, :] = totals[a].astype(BF16)

    pieces = [
        (end, n, which, base) for end in range(2) for n in range(RANGE) for which in range(2) for base in range(0, count, 2 * SUB)
    ]

    tile_shape = (count, cols)
    spot = lane_index((1, cols)) % TAPS
    spots = lane_index(tile_shape) % TAPS
    for tile in range(rows // group):
        mine = own[tile].astype(F32)
        theirs = side[tile, 2 * count :, :].astype(F32)
        for which in range(2):
            packed = side[tile, which * count : (which + 1) * count, :]
            total = {}
            for k in range(1, RANGE + 1):
                moved = jnp.where(spots < RANGE, pltpu.roll(packed, LANES - k, 1), pltpu.roll(packed, k, 1)).astype(F32)
                for a in ODD:
                    slot = ODD.index(a) * TAPS + k - 1
                    if which == 0:
                        tops, bottoms = mine[slot : slot + 1], mine[slot + RANGE : slot + RANGE + 1]
                        weight = jnp.where(spot < RANGE, tops * scale_of(a, k - 1), bottoms * scale_of(a, RANGE + k - 1))
                    else:
                        tops = pltpu.roll(theirs, LANES - k, 1)[slot + RANGE : slot + RANGE + 1]
                        bottoms = pltpu.roll(theirs, k, 1)[slot : slot + 1]
                        weight = jnp.where(spot < RANGE, tops * scale_of(a, RANGE + k - 1), bottoms * scale_of(a, k - 1))
                    valid = ((spot < RANGE) & (spot + k >= RANGE)) | ((spot >= RANGE) & (spot - k < RANGE))
                    term = jnp.where(valid, weight, 0.0) * moved
                    total[a] = term if k == 1 else total[a] + term
            for a in ODD:
                band[which, ODD.index(a), tile] = total[a].astype(BF16)

    acc[...] = jnp.zeros_like(acc)
    rim_lane = (lane_index(tile_shape) < RANGE) | (lane_index(tile_shape) >= cols - RANGE)
    rim = jnp.where(rim_lane, 1.0, 0.0).astype(BF16)

    def results(row, even_of):
        found = []
        tile = row // group
        turn = (2 * LANES - RANGE - TAPS * (row % group)) % LANES
        for which in range(2):
            both = along[which, row]
            done = {a: even_of(which)[EVEN.index(a) * count : (EVEN.index(a) + 1) * count] for a in EVEN}
            for o, a in enumerate(ODD):
                beyond = (pltpu.roll(band[which, o, tile], turn, 1) * rim).astype(F32)
                done[a] = (both[:, o * cols : (o + 1) * cols] + beyond).astype(BF16)
            found.append(jnp.concatenate([done[a] for a in range(OPS)], axis=0))
        return found

    def accumulate(pair):
        found = [results(*one) for one in pair]
        first = jnp.concatenate([one[0] for one in found], axis=1)
        back = jnp.concatenate([one[1] for one in found], axis=1)
        acc[...] += lax.dot_general(back, first, (((1,), (1,)), ((), ())), preferred_element_type=F32)

    def end_row(n):
        return (n if n < RANGE else rows - 2 * RANGE + n), lambda which: ends[which, n]

    def inner_row(row):
        return row, lambda which: inner[which, row]

    middle_rows = range(RANGE, rows - RANGE, 2)
    for n, row in enumerate(middle_rows):
        for piece in pieces[n * len(pieces) // len(middle_rows) : (n + 1) * len(pieces) // len(middle_rows)]:
            end_piece(*piece)
        accumulate([inner_row(row), inner_row(row + 1)])
    for n in range(0, 2 * RANGE, 2):
        accumulate([end_row(n), end_row(n + 1)])

    parts_left, parts_right = widths
    per_left, per_right = count // parts_left, count // parts_right
    moved = jnp.dot(orders[0], acc[...].astype(BF16), preferred_element_type=F32).astype(BF16)
    moved = jnp.dot(moved, orders[1], preferred_element_type=F32).astype(BF16)
    if out.ndim == 2:
        out[...] = moved
    else:
        width = OPS * per_right
        for d in range(parts_left * parts_right):
            w, r = divmod(d, parts_right)
            out[d] = moved[w * OPS * per_left : (w + 1) * OPS * per_left, r * width : (r + 1) * width]


def sum_kernel(factor, got, out):
    total = jnp.sum(got[...].astype(F32), axis=0) * factor
    per_left, per_right = out.shape[1], out.shape[2]
    for a in range(OPS):
        for b in range(OPS):
            out[a * OPS + b] = total[a * per_left : (a + 1) * per_left, b * per_right : (b + 1) * per_right]


def swap(array, axis, pairs):
    return lax.ppermute(array, axis, pairs)


def on_device(left, right, bond_signs, hop):
    count, rows, cols = right.shape
    wide, narrow = lax.axis_size("wide"), lax.axis_size("narrow")
    edge_rows = 2 * count + len(EVEN) * TAPS
    side_rows = 2 * count + len(ODD) * TAPS
    tiles = rows * TAPS // LANES
    parity = (lax.axis_index("wide") % 2).astype(jnp.int32).reshape(1)
    smem = pl.BlockSpec(memory_space=pltpu.SMEM)
    vmem = pl.BlockSpec(memory_space=pltpu.VMEM)
    params = pltpu.CompilerParams(vmem_limit_bytes=VMEM_LIMIT)

    hbm = pl.BlockSpec(memory_space=pltpu.HBM)

    near, far, side, own, value, coef, orders = pl.pallas_call(
        lambda *refs: pack_kernel((wide, narrow), *refs),
        out_shape=(
            jax.ShapeDtypeStruct((RANGE, edge_rows, cols), BF16),
            jax.ShapeDtypeStruct((RANGE, edge_rows, cols), BF16),
            jax.ShapeDtypeStruct((tiles, side_rows, cols), BF16),
            jax.ShapeDtypeStruct((tiles, side_rows - 2 * count, cols), BF16),
            jax.ShapeDtypeStruct((2, (count + SUB) * (rows + 1), cols), F32),
            jax.ShapeDtypeStruct((OPS * TAPS, rows + 2 * SUB, cols), F32),
            jax.ShapeDtypeStruct((2, OPS * count, OPS * count), BF16),
        ),
        in_specs=[smem, hbm, hbm, hbm, hbm],
        out_specs=(vmem,) * 7,
        scratch_shapes=[
            pltpu.SMEM((OPS, RANGE), F32),
            VMEM((2, count, rows, cols), BF16),
            VMEM((OPS, TAPS, rows, cols), jnp.int32),
            VMEM((3 * SUB * (rows + 1), cols), F32),
            VMEM((edge_rows * SUB + SUB, cols), F32),
            VMEM((edge_rows * SUB + SUB, cols), F32),
            pltpu.SemaphoreType.DMA((2 * (count // (2 * SUB)) + OPS + 1,)),
        ],
        compiler_params=params,
        name="pack",
    )(parity, *(pltpu.with_memory_space_constraint(one, pltpu.HBM) for one in (hop, right, left, bond_signs)))
    inner, along = pl.pallas_call(
        inner_kernel,
        out_shape=(
            jax.ShapeDtypeStruct((2, rows, len(EVEN) * count, cols), BF16),
            jax.ShapeDtypeStruct((2, rows, count, len(ODD) * cols), F32),
        ),
        in_specs=[vmem, vmem],
        out_specs=(vmem,) * 2,
        compiler_params=params,
        name="interior",
    )(value, coef)

    far = swap(far, "wide", [(i, (i + 1) % wide if i % 2 else (i - 1) % wide) for i in range(wide)])
    near = swap(near, "wide", [(i, i ^ 1) for i in range(wide)])
    if narrow == 2:
        side = swap(side, "narrow", [(0, 1), (1, 0)])
    else:
        before = swap(side, "narrow", [(i, (i + 1) % narrow) for i in range(narrow)])
        after = swap(side, "narrow", [((i + 1) % narrow, i) for i in range(narrow)])
        side = jnp.where(lane_index(side.shape) % TAPS < RANGE, before, after)

    per_left, per_right = count // wide, count // narrow
    size = OPS * count
    direct = (OPS * per_right) % LANES == 0 and (OPS * per_left) % 16 == 0
    blocked = (wide * narrow, OPS * per_left, OPS * per_right)
    partial = pl.pallas_call(
        lambda *refs: main_kernel((wide, narrow), *refs),
        out_shape=jax.ShapeDtypeStruct(blocked if direct else (size, size), BF16),
        in_specs=[smem, smem] + [vmem] * 9,
        out_specs=vmem,
        scratch_shapes=[
            VMEM((2, len(ODD), tiles, count, cols), BF16),
            VMEM((2, RANGE, edge_rows, cols), BF16),
            VMEM((len(EVEN) * TAPS, RANGE + 2 * SUB, cols), F32),
            VMEM((2, 2 * RANGE, len(EVEN) * count, cols), BF16),
            VMEM((size, size), F32),
        ],
        compiler_params=params,
        name="moments",
    )(parity, hop, coef, value, inner, along, near, far, side, own, orders)
    if not direct:
        partial = partial.reshape(wide, OPS * per_left, narrow, OPS * per_right).transpose(0, 2, 1, 3).reshape(blocked)
    got = lax.all_to_all(partial, ("wide", "narrow"), 0, 0, tiled=True)
    factor = 1.0 / math.sqrt(rows * cols * wide * narrow)
    return pl.pallas_call(
        lambda *refs: sum_kernel(factor, *refs),
        out_shape=jax.ShapeDtypeStruct((OPS * OPS, per_left, per_right), F32),
        in_specs=[vmem],
        out_specs=vmem,
        compiler_params=params,
        name="total",
    )(got)


def solution(mesh):
    in_specs = (
        P(None, "wide", "narrow"),
        P(None, "wide", "narrow"),
        P(None, None, "wide", "narrow"),
        P(),
    )
    out_specs = P(None, "wide", "narrow")

    return jax.shard_map(on_device, mesh=mesh, in_specs=in_specs, out_specs=out_specs, check_vma=False)
```

```python
import math

import jax
import jax.numpy as jnp
from jax import lax
from jax.experimental import pallas as pl
from jax.experimental.pallas import tpu as pltpu
from jax.sharding import PartitionSpec as P


OPS = 4
RANGE = 4
TAPS = 2 * RANGE
EVEN = tuple(a for a in range(OPS) if a % 2 == 0)
ODD = tuple(a for a in range(OPS) if a % 2 == 1)
SUB = 8
LANES = 128
VMEM = pltpu.VMEM
F32 = jnp.float32
BF16 = jnp.bfloat16
INNER_BODY = 28
INNER_LEAD = 6
VMEM_LIMIT = 24 * 1024 * 1024


def lane_index(shape):
    return lax.broadcasted_iota(jnp.int32, shape, len(shape) - 1)


def pack_kernel(widths, parity, hop_far, right, left, bonds, near, far, side, own, value, coef, orders, hop, vectors, bits, flat, head, tail, sems):
    count, rows, cols = right.shape
    even = parity[0] == 0
    group = LANES // TAPS
    pitch = rows + 1
    batch = 2 * SUB
    batches = count // batch

    copies = []
    for which, ref in enumerate((right, left)):
        for n in range(batches):
            copies.append((ref.at[pl.ds(n * batch, batch)], vectors.at[which, pl.ds(n * batch, batch)]))
    for a in ODD + EVEN:
        copies.append((bonds.at[a], bits.at[a]))
    copies.append((hop_far, hop))
    copies = [pltpu.make_async_copy(src, dst, sems.at[n]) for n, (src, dst) in enumerate(copies)]
    for copy in copies[:batches] + copies[2 * batches :] + copies[batches : 2 * batches]:
        copy.start()

    size = OPS * count

    def order(parts, dim):
        per = count // parts
        new = lax.broadcasted_iota(jnp.int32, (size, size), dim)
        old = lax.broadcasted_iota(jnp.int32, (size, size), 1 - dim)
        part, rest = new // (OPS * per), new % (OPS * per)
        return jnp.where(old == (rest // per) * count + part * per + rest % per, 1.0, 0.0).astype(BF16)

    for dim in range(2):
        orders[dim] = order(widths[dim], dim)

    lane = lane_index((batch, cols)) // TAPS

    def pack(at, flat):
        for tile in range(rows // group):
            total = jnp.zeros((batch, cols), F32)
            for r in range(group):
                row = tile * group + r
                strip = jnp.concatenate(
                    [flat[pl.ds(half * SUB * pitch + row, SUB, stride=pitch), :] for half in range(2)], axis=0
                )
                total = jnp.where(lane == r, pltpu.roll(strip, (RANGE + TAPS * r) % LANES, 1), total)
            side[tile, at : at + batch, :] = total.astype(BF16)

    def send(at):
        for row in range(RANGE):
            def strip(ref, offset):
                parts = [ref[pl.ds((at + half * SUB) * SUB + offset, SUB, stride=SUB), :] for half in range(2)]
                return jnp.concatenate(parts, axis=0)

            low = strip(head, row)
            high = strip(tail, SUB - RANGE + row)
            near[row, at : at + batch, :] = jnp.where(even, high, low).astype(BF16)
            far[row, at : at + batch, :] = jnp.where(even, low, high).astype(BF16)

    def vectors_of(which, together):
        for n in range(batches):
            for m in range(n, n + together if n % together == 0 else n):
                copies[which * batches + m].wait()
            at = which * count + n * batch
            for v in range(batch):
                one = vectors[which, n * batch + v].astype(F32)
                start = (n * batch + v) * pitch
                value[which, start : start + rows, :] = one
                head[(at + v) * SUB : (at + v + 1) * SUB, :] = one[:SUB]
                tail[(at + v) * SUB : (at + v + 1) * SUB, :] = one[rows - SUB :]
            pack(at, value.at[which, pl.ds(n * batch * pitch, (batch + SUB) * pitch)])
            send(at)

    vectors_of(0, batches)
    at = 2 * count
    copies[-1].wait()
    for n, a in enumerate(ODD + EVEN):
        copies[2 * batches + n].wait()
        for index in range(TAPS):
            scale = hop[a, index % RANGE] * (1.0 if index < RANGE else -1.0)
            sign = (2 * bits[a, index] - 1).astype(F32)
            coef[a * TAPS + index, :rows, :] = sign * scale
            if a in ODD:
                t = ODD.index(a) * TAPS + index
                flat[t * pitch : t * pitch + rows, :] = sign
            else:
                t = at + EVEN.index(a) * TAPS + index
                head[t * SUB : (t + 1) * SUB, :] = sign[:SUB]
                tail[t * SUB : (t + 1) * SUB, :] = sign[rows - SUB :]
    pack(at, flat)
    send(at)
    vectors_of(1, batches)
    own[...] = side[:, at:, :]


def along_rows(which, value_at, factor_at):
    totals = {}
    for index in range(TAPS):
        step = (index % RANGE + 1) * (1 if index < RANGE else -1) * (1 if which == 0 else -1)
        moved = value_at(step)
        for a in EVEN:
            term = factor_at(a, index) * moved
            totals[a] = term if index == 0 else totals[a] + term
    return totals


def factor_row(which, row, index):
    step = index % RANGE + 1
    return row if which == 0 else row + (-step if index < RANGE else step)


def inner_kernel(value, coef, inner, along):
    _, rows, count, _ = along.shape
    cols = coef.shape[2]
    pitch = rows + 1
    period = 2 * TAPS

    tile = (period, cols)
    gap = (lane_index(tile) - lax.broadcasted_iota(jnp.int32, tile, 0)) % period
    near_diagonal = lane_index((cols, cols)) - lax.broadcasted_iota(jnp.int32, (cols, cols), 0)
    within = jnp.where((near_diagonal >= -TAPS) & (near_diagonal < TAPS), 1.0, 0.0).astype(BF16)

    def matrices(row):
        pieces = {}
        for a in ODD:
            total = jnp.zeros(tile, F32)
            for k in range(1, RANGE + 1):
                total = jnp.where(gap == period - k, coef[a * TAPS + k - 1, pl.ds(row, period, stride=0), :], total)
                total = jnp.where(gap == k, coef[a * TAPS + RANGE + k - 1, pl.ds(row, period, stride=0), :], total)
            high = total.astype(BF16)
            low = (total - high.astype(F32)).astype(BF16)
            for part, piece in enumerate((high, low)):
                pieces[part, a] = jnp.concatenate([piece] * (cols // period), axis=0) * within
        right_side = jnp.concatenate([jnp.concatenate([pieces[part, a] for a in ODD], axis=1) for part in range(2)], axis=0)
        left_side = jnp.concatenate([jnp.concatenate([pieces[part, a] for part in range(2)], axis=1) for a in ODD], axis=0)
        return right_side, left_side

    def strip(which, g, row):
        return value[which, pl.ds(g * SUB * pitch + row, SUB, stride=pitch), :]

    def columns(row):
        bands = matrices(row)
        for which in range(2):
            middle = jnp.concatenate([strip(which, g, row) for g in range(count // SUB)], axis=0).astype(BF16)
            middle = jnp.concatenate([middle, middle], axis=1)
            dims = (((1,), (which,)), ((), ()))
            along[which, row] = lax.dot_general(middle, bands[which], dims, preferred_element_type=F32)

    def lines(row):
        for which in range(2):
            factors = {}
            for a in EVEN:
                for index in range(TAPS):
                    factors[a, index] = coef[a * TAPS + index, pl.ds(factor_row(which, row, index), SUB, stride=0), :]
            for pair in range(count // (2 * SUB)):
                halves = [
                    along_rows(which, lambda step, g=2 * pair + half: strip(which, g, row + step), lambda a, index: factors[a, index])
                    for half in range(2)
                ]
                for o, a in enumerate(EVEN):
                    at = o * count + pair * 2 * SUB
                    inner[which, row, at : at + 2 * SUB, :] = jnp.concatenate([half[a] for half in halves], axis=0).astype(BF16)

    trips = (rows - 2 * RANGE) // INNER_BODY
    each = rows // trips

    @pl.loop(0, trips)
    def _(step):
        for n in range(each):
            columns(step * each + n)
            if n >= INNER_LEAD:
                lines(RANGE + step * INNER_BODY + n - INNER_LEAD)
        for n in range(each - INNER_LEAD, INNER_BODY):
            lines(RANGE + step * INNER_BODY + n)


def main_kernel(widths, parity, hop, coef, value, inner, along, near, far, side, own, orders, out, band, beyond_rows, near_ends, ends, acc):
    _, rows, count, _ = along.shape
    cols = coef.shape[2]
    pitch = rows + 1
    even = parity[0] == 0
    group = LANES // TAPS

    def scale_of(a, index):
        return hop[a, index % RANGE] * (1.0 if index < RANGE else -1.0)

    beyond_rows[0] = jnp.where(even, far[...], near[...])
    beyond_rows[1] = jnp.where(even, near[...], far[...])

    def outer(slab, row):
        return [beyond_rows[end, row, slab, :].astype(F32) for end in range(2)]

    for row in range(RANGE):
        low, high = outer(slice(2 * count, 2 * count + 2 * SUB), row)
        for slot in range(len(EVEN) * TAPS):
            a, index = EVEN[slot // TAPS], slot % TAPS
            source = low if index < RANGE else high
            near_ends[slot, row : row + 1, :] = source[slot : slot + 1] * scale_of(a, index)

    def end_piece(end, n, which, base):
        row = n if end == 0 else rows - RANGE + n
        slab = slice(which * count + base, which * count + base + 2 * SUB)

        def value_at(step):
            at = row + step
            if at < 0:
                return outer(slab, at + RANGE)[0]
            if at >= rows:
                return outer(slab, at - rows)[1]
            parts = [value[which, pl.ds((base + half * SUB) * pitch + at, SUB, stride=pitch), :] for half in range(2)]
            return jnp.concatenate(parts, axis=0)

        def factor_at(a, index):
            at = factor_row(which, row, index)
            if 0 <= at < rows:
                return coef[a * TAPS + index, pl.ds(at, 2 * SUB, stride=0), :]
            at = at + RANGE if at < 0 else at - rows
            return near_ends[EVEN.index(a) * TAPS + index, pl.ds(at, 2 * SUB, stride=0), :]

        totals = along_rows(which, value_at, factor_at)
        for o, a in enumerate(EVEN):
            at = o * count + base
            ends[which, end * RANGE + n, at : at + 2 * SUB, :] = totals[a].astype(BF16)

    pieces = [
        (end, n, which, base) for end in range(2) for n in range(RANGE) for which in range(2) for base in range(0, count, 2 * SUB)
    ]

    tile_shape = (count, cols)
    spot = lane_index((1, cols)) % TAPS
    spots = lane_index(tile_shape) % TAPS
    for tile in range(rows // group):
        mine = own[tile].astype(F32)
        theirs = side[tile, 2 * count :, :].astype(F32)
        for which in range(2):
            packed = side[tile, which * count : (which + 1) * count, :]
            total = {}
            for k in range(1, RANGE + 1):
                moved = jnp.where(spots < RANGE, pltpu.roll(packed, LANES - k, 1), pltpu.roll(packed, k, 1)).astype(F32)
                for a in ODD:
                    slot = ODD.index(a) * TAPS + k - 1
                    if which == 0:
                        tops, bottoms = mine[slot : slot + 1], mine[slot + RANGE : slot + RANGE + 1]
                        weight = jnp.where(spot < RANGE, tops * scale_of(a, k - 1), bottoms * scale_of(a, RANGE + k - 1))
                    else:
                        tops = pltpu.roll(theirs, LANES - k, 1)[slot + RANGE : slot + RANGE + 1]
                        bottoms = pltpu.roll(theirs, k, 1)[slot : slot + 1]
                        weight = jnp.where(spot < RANGE, tops * scale_of(a, RANGE + k - 1), bottoms * scale_of(a, k - 1))
                    valid = ((spot < RANGE) & (spot + k >= RANGE)) | ((spot >= RANGE) & (spot - k < RANGE))
                    term = jnp.where(valid, weight, 0.0) * moved
                    total[a] = term if k == 1 else total[a] + term
            for a in ODD:
                band[which, ODD.index(a), tile] = total[a].astype(BF16)

    acc[...] = jnp.zeros_like(acc)
    rim_lane = (lane_index(tile_shape) < RANGE) | (lane_index(tile_shape) >= cols - RANGE)
    rim = jnp.where(rim_lane, 1.0, 0.0).astype(BF16)

    def results(row, even_of):
        found = []
        tile = row // group
        turn = (2 * LANES - RANGE - TAPS * (row % group)) % LANES
        for which in range(2):
            both = along[which, row]
            done = {a: even_of(which)[EVEN.index(a) * count : (EVEN.index(a) + 1) * count] for a in EVEN}
            for o, a in enumerate(ODD):
                beyond = (pltpu.roll(band[which, o, tile], turn, 1) * rim).astype(F32)
                done[a] = (both[:, o * cols : (o + 1) * cols] + beyond).astype(BF16)
            found.append(jnp.concatenate([done[a] for a in range(OPS)], axis=0))
        return found

    def accumulate(pair):
        found = [results(*one) for one in pair]
        first = jnp.concatenate([one[0] for one in found], axis=1)
        back = jnp.concatenate([one[1] for one in found], axis=1)
        acc[...] += lax.dot_general(back, first, (((1,), (1,)), ((), ())), preferred_element_type=F32)

    def end_row(n):
        return (n if n < RANGE else rows - 2 * RANGE + n), lambda which: ends[which, n]

    def inner_row(row):
        return row, lambda which: inner[which, row]

    middle_rows = range(RANGE, rows - RANGE, 2)
    for n, row in enumerate(middle_rows):
        for piece in pieces[n * len(pieces) // len(middle_rows) : (n + 1) * len(pieces) // len(middle_rows)]:
            end_piece(*piece)
        accumulate([inner_row(row), inner_row(row + 1)])
    for n in range(0, 2 * RANGE, 2):
        accumulate([end_row(n), end_row(n + 1)])

    parts_left, parts_right = widths
    per_left, per_right = count // parts_left, count // parts_right
    moved = jnp.dot(orders[0], acc[...].astype(BF16), preferred_element_type=F32).astype(BF16)
    moved = jnp.dot(moved, orders[1], preferred_element_type=F32).astype(BF16)
    if out.ndim == 2:
        out[...] = moved
    else:
        width = OPS * per_right
        for d in range(parts_left * parts_right):
            w, r = divmod(d, parts_right)
            out[d] = moved[w * OPS * per_left : (w + 1) * OPS * per_left, r * width : (r + 1) * width]


def sum_kernel(factor, got, out):
    total = jnp.sum(got[...].astype(F32), axis=0) * factor
    per_left, per_right = out.shape[1], out.shape[2]
    for a in range(OPS):
        for b in range(OPS):
            out[a * OPS + b] = total[a * per_left : (a + 1) * per_left, b * per_right : (b + 1) * per_right]


def swap(array, axis, pairs):
    return lax.ppermute(array, axis, pairs)


def on_device(left, right, bond_signs, hop):
    count, rows, cols = right.shape
    wide, narrow = lax.axis_size("wide"), lax.axis_size("narrow")
    edge_rows = 2 * count + len(EVEN) * TAPS
    side_rows = 2 * count + len(ODD) * TAPS
    tiles = rows * TAPS // LANES
    parity = (lax.axis_index("wide") % 2).astype(jnp.int32).reshape(1)
    smem = pl.BlockSpec(memory_space=pltpu.SMEM)
    vmem = pl.BlockSpec(memory_space=pltpu.VMEM)
    params = pltpu.CompilerParams(vmem_limit_bytes=VMEM_LIMIT)

    hbm = pl.BlockSpec(memory_space=pltpu.HBM)

    near, far, side, own, value, coef, orders = pl.pallas_call(
        lambda *refs: pack_kernel((wide, narrow), *refs),
        out_shape=(
            jax.ShapeDtypeStruct((RANGE, edge_rows, cols), BF16),
            jax.ShapeDtypeStruct((RANGE, edge_rows, cols), BF16),
            jax.ShapeDtypeStruct((tiles, side_rows, cols), BF16),
            jax.ShapeDtypeStruct((tiles, side_rows - 2 * count, cols), BF16),
            jax.ShapeDtypeStruct((2, (count + SUB) * (rows + 1), cols), F32),
            jax.ShapeDtypeStruct((OPS * TAPS, rows + 2 * SUB, cols), F32),
            jax.ShapeDtypeStruct((2, OPS * count, OPS * count), BF16),
        ),
        in_specs=[smem, hbm, hbm, hbm, hbm],
        out_specs=(vmem,) * 7,
        scratch_shapes=[
            pltpu.SMEM((OPS, RANGE), F32),
            VMEM((2, count, rows, cols), BF16),
            VMEM((OPS, TAPS, rows, cols), jnp.int32),
            VMEM((3 * SUB * (rows + 1), cols), F32),
            VMEM((edge_rows * SUB + SUB, cols), F32),
            VMEM((edge_rows * SUB + SUB, cols), F32),
            pltpu.SemaphoreType.DMA((2 * (count // (2 * SUB)) + OPS + 1,)),
        ],
        compiler_params=params,
        name="pack",
    )(parity, *(pltpu.with_memory_space_constraint(one, pltpu.HBM) for one in (hop, right, left, bond_signs)))
    inner, along = pl.pallas_call(
        inner_kernel,
        out_shape=(
            jax.ShapeDtypeStruct((2, rows, len(EVEN) * count, cols), BF16),
            jax.ShapeDtypeStruct((2, rows, count, len(ODD) * cols), F32),
        ),
        in_specs=[vmem, vmem],
        out_specs=(vmem,) * 2,
        compiler_params=params,
        name="interior",
    )(value, coef)

    far = swap(far, "wide", [(i, (i + 1) % wide if i % 2 else (i - 1) % wide) for i in range(wide)])
    near = swap(near, "wide", [(i, i ^ 1) for i in range(wide)])
    if narrow == 2:
        side = swap(side, "narrow", [(0, 1), (1, 0)])
    else:
        before = swap(side, "narrow", [(i, (i + 1) % narrow) for i in range(narrow)])
        after = swap(side, "narrow", [((i + 1) % narrow, i) for i in range(narrow)])
        side = jnp.where(lane_index(side.shape) % TAPS < RANGE, before, after)

    per_left, per_right = count // wide, count // narrow
    size = OPS * count
    direct = (OPS * per_right) % LANES == 0 and (OPS * per_left) % 16 == 0
    blocked = (wide * narrow, OPS * per_left, OPS * per_right)
    partial = pl.pallas_call(
        lambda *refs: main_kernel((wide, narrow), *refs),
        out_shape=jax.ShapeDtypeStruct(blocked if direct else (size, size), BF16),
        in_specs=[smem, smem] + [vmem] * 9,
        out_specs=vmem,
        scratch_shapes=[
            VMEM((2, len(ODD), tiles, count, cols), BF16),
            VMEM((2, RANGE, edge_rows, cols), BF16),
            VMEM((len(EVEN) * TAPS, RANGE + 2 * SUB, cols), F32),
            VMEM((2, 2 * RANGE, len(EVEN) * count, cols), BF16),
            VMEM((size, size), F32),
        ],
        compiler_params=params,
        name="moments",
    )(parity, hop, coef, value, inner, along, near, far, side, own, orders)
    if not direct:
        partial = partial.reshape(wide, OPS * per_left, narrow, OPS * per_right).transpose(0, 2, 1, 3).reshape(blocked)
    got = lax.all_to_all(partial, ("wide", "narrow"), 0, 0, tiled=True)
    factor = 1.0 / math.sqrt(rows * cols * wide * narrow)
    return pl.pallas_call(
        lambda *refs: sum_kernel(factor, *refs),
        out_shape=jax.ShapeDtypeStruct((OPS * OPS, per_left, per_right), F32),
        in_specs=[vmem],
        out_specs=vmem,
        compiler_params=params,
        name="total",
    )(got)


def solution(mesh):
    in_specs = (
        P(None, "wide", "narrow"),
        P(None, "wide", "narrow"),
        P(None, None, "wide", "narrow"),
        P(),
    )
    out_specs = P(None, "wide", "narrow")

    return jax.shard_map(on_device, mesh=mesh, in_specs=in_specs, out_specs=out_specs, check_vma=False)
```
